256 devices in a mesh: ctx: 8 (over z), head: 4 (over y_hi, core), sess: 8 (over y_lo, x).
Axes of the slice: x: 4, y: 4 (y_hi: 2, y_lo: 2; y = y_hi * 2 + y_lo), z: 8, core: 2. Of those that a mesh axis runs over, the one named last changes fastest.
Arguments:
- queries: bfloat16 [512, 64, 128], P(('ctx', 'sess'), 'head'), may hold values from -300 to 300
- prefix_keys: bfloat16 [8, 49152, 128], P('head', 'ctx'), may hold values from -5 to 5
- prefix_values: bfloat16 [8, 49152, 128], P('head', 'ctx'), may hold values from -6 to 6
- suffix_keys: bfloat16 [512, 8, 512, 128], P(('ctx', 'sess'), 'head'), may hold values from -7 to 7
- suffix_values: bfloat16 [512, 8, 512, 128], P(('ctx', 'sess'), 'head'), may hold values from -6 to 6
- lengths: int32 [512], P(('ctx', 'sess')), may hold values from 1 to 512, as said below
- out_weight: bfloat16 [8192, 8192], P('head', ('ctx', 'sess')), may hold values from -0.0625 to 0.0625
Outputs:
- layer_out: float32 [512, 8192], P('head', ('ctx', 'sess'))
The draws below stay inside these ranges and needn't reach their ends.
Inputs may be any that keep to these rules, and one draw needn't show every extreme that they name: `lengths`: every session has at least one live suffix token; some session has exactly 512.
All inputs are finite; a program needn't handle non-finite values.
Results may differ from the reference program's by a relative error of at most 0.0065.
Values may be sent and summed in bfloat16 or wider, within the bound.
No kernel may reach another device: no remote copies, remote signals or barrier semaphores. Data moves between devices by JAX's collectives and lax.ppermute only.
A program may use at most 64 MiB of HBM per device.

```python
import math
import jax
import jax.numpy as jnp
from jax import lax

D = 8192
QH = 64
KVH = 8
HD = 128
SUF = 512
SESS = 512
PREFIX = 49152


def draw_prefix_keys(key, part):
    noise_key = jax.random.fold_in(key, 11)
    base = jnp.clip(jax.random.normal(noise_key, (KVH, PREFIX, HD), jnp.float32), -5.0, 5.0)
    return base.astype(jnp.bfloat16)


def draw_queries(key, part):
    noise_key = jax.random.fold_in(key, 23)
    base = 3.0 * jnp.clip(jax.random.normal(noise_key, (SESS, QH, HD), jnp.float32), -6.0, 6.0)
    return base.astype(jnp.bfloat16)


def draw_lengths(key, part):
    long_pick = jax.random.randint(jax.random.fold_in(key, 31), (SESS,), 0, 8) == 0
    long_len = jax.random.randint(jax.random.fold_in(key, 32), (SESS,), SUF // 2, SUF + 1)
    short_len = jax.random.randint(jax.random.fold_in(key, 33), (SESS,), 1, SUF // 4 + 1)
    chosen = jnp.where(long_pick, long_len, short_len)
    target = jax.random.randint(jax.random.fold_in(key, 34), (), 0, SESS)
    return jnp.where(jnp.arange(SESS, dtype=jnp.int32) == target, SUF, chosen).astype(jnp.int32)


def steps_of(own_key, dims, cuts, smallest, top_value):
    gain, own = 1.0, jax.random.fold_in(own_key, 6)
    for dim, parts in cuts:
        steps = jnp.exp(jax.random.uniform(jax.random.fold_in(own, dim), (parts,), jnp.float32, smallest / len(cuts), top_value / len(cuts)))
        gain = gain * jnp.repeat(steps, dims[dim] // parts).reshape([-1 if axis == dim else 1 for axis in range(len(dims))])
    return gain


def normal_values(rng, shape, spread, reach, cuts=(), held_as=jnp.bfloat16):
    values = spread * jax.random.normal(rng, shape, jnp.float32)
    if cuts:
        values = values * steps_of(rng, shape, cuts, -0.22, 0.18)
    return jnp.clip(values, -reach, reach).astype(held_as)


def setup_inputs(seed: int = 0) -> dict:
    key_of = jax.random.split(jax.random.key(seed), 8)
    queries = draw_queries(jax.random.fold_in(key_of[7], 71), 0)
    prefix_keys = draw_prefix_keys(jax.random.fold_in(key_of[7], 71), 0)
    prefix_values = normal_values(key_of[2], (KVH, PREFIX, HD), 1.0, 6.0, ((0, 4), (1, 8)))
    suffix_keys = normal_values(key_of[3], (SESS, KVH, SUF, HD), 1.3, 7.0, ((0, 64), (1, 4)))
    suffix_values = normal_values(key_of[4], (SESS, KVH, SUF, HD), 1.0, 6.0, ((0, 64), (1, 4)))
    lengths = draw_lengths(jax.random.fold_in(key_of[7], 71), 0)
    out_weight = normal_values(key_of[6], (QH * HD, D), (QH * HD) ** -0.5, 0.0625, ((0, 4), (1, 64)))
    return {"queries": queries, "prefix_keys": prefix_keys, "prefix_values": prefix_values, "suffix_keys": suffix_keys, "suffix_values": suffix_values, "lengths": lengths, "out_weight": out_weight}


def reference(queries, prefix_keys, prefix_values, suffix_keys, suffix_values, lengths, out_weight):
    group_size = QH // KVH
    score_scale = 1.0 / math.sqrt(HD)
    rows_block = 8
    prefix_k32 = prefix_keys.astype(jnp.float32)
    prefix_v32 = prefix_values.astype(jnp.float32)

    def one_block(block_index):
        first_row = (block_index * rows_block).astype(jnp.int32)
        query_block = lax.dynamic_slice_in_dim(queries, first_row, rows_block, 0).astype(jnp.float32)
        query_block = query_block.reshape(rows_block, KVH, group_size, HD)
        suffix_k = lax.dynamic_slice_in_dim(suffix_keys, first_row, rows_block, 0).astype(jnp.float32)
        suffix_v = lax.dynamic_slice_in_dim(suffix_values, first_row, rows_block, 0).astype(jnp.float32)
        live_len = lax.dynamic_slice_in_dim(lengths, first_row, rows_block, 0)
        prefix_scores = jnp.einsum('skgd,knd->skgn', query_block, prefix_k32) * score_scale
        suffix_scores = jnp.einsum('skgd,sknd->skgn', query_block, suffix_k) * score_scale
        position = jnp.arange(SUF, dtype=jnp.int32)
        live_mask = position[None, :] < live_len[:, None]
        suffix_scores = jnp.where(live_mask[:, None, None, :], suffix_scores, -1e+30)
        row_top = jnp.maximum(lax.optimization_barrier(jnp.max(prefix_scores, axis=-1)), lax.optimization_barrier(jnp.max(suffix_scores, axis=-1)))
        prefix_weights = jnp.exp(prefix_scores - row_top[..., None])
        suffix_weights = jnp.exp(suffix_scores - row_top[..., None])
        total = lax.optimization_barrier(jnp.sum(prefix_weights, axis=-1)) + lax.optimization_barrier(jnp.sum(suffix_weights, axis=-1))
        numerator = jnp.einsum('skgn,knd->skgd', prefix_weights.astype(jnp.bfloat16).astype(jnp.float32), prefix_v32)
        numerator = numerator + jnp.einsum('skgn,sknd->skgd', suffix_weights.astype(jnp.bfloat16).astype(jnp.float32), suffix_v)
        attended = (numerator / total[..., None]).astype(jnp.bfloat16)
        return attended.reshape(rows_block, QH * HD)
    attended = lax.map(one_block, jnp.arange(SESS // rows_block, dtype=jnp.int32))
    attended = attended.reshape(SESS, QH * HD)
    return jnp.dot(attended, out_weight, preferred_element_type=jnp.float32)
```

```python
import functools
import math

import jax
import jax.numpy as jnp
from jax import lax
from jax.experimental import pallas as pl
from jax.experimental.pallas import tpu as pltpu
from jax.sharding import Mesh
from jax.sharding import PartitionSpec as P

F32 = jnp.float32
BF16 = jnp.bfloat16
LOG2E = 1.4426950408889634
HEAD = ("yh", "core")
SESS = ("yl", "x")
NT = (((1,), (1,)), ((), ()))


def prefix_kernel(scale, q_ref, k_ref, v_ref, o_ref, m_ref, l_ref, acc_ref, lse_ref):
    head, block = pl.program_id(0), pl.program_id(1)
    last = pl.num_programs(1) - 1
    sources, heads, rows, dim = q_ref.shape

    @pl.when(block == 0)
    def _():
        m_ref[...] = jnp.full_like(m_ref, -1e30)
        l_ref[...] = jnp.zeros_like(l_ref)
        acc_ref[...] = jnp.zeros_like(acc_ref)

    chunk = 2
    k = k_ref[0]
    v = v_ref[0]
    for first in range(0, sources, chunk):
        span = pl.ds(first * rows, chunk * rows)
        q = q_ref[pl.ds(first, chunk), head].reshape(chunk * rows, dim)
        scores = lax.dot_general(q, k, NT, preferred_element_type=F32)
        old = m_ref[span, 0:1]
        new = jnp.maximum(old, jnp.max(scores, axis=1, keepdims=True))
        factor = jnp.exp2((old - new) * scale)
        weights = jnp.exp2((scores - new) * scale)
        l_ref[span, 0:1] = l_ref[span, 0:1] * factor + jnp.sum(weights, axis=1, keepdims=True)
        m_ref[span, 0:1] = new
        acc_ref[span, :] = acc_ref[span, :] * factor + jnp.dot(
            weights.astype(BF16), v, preferred_element_type=F32
        )

    @pl.when(block == last)
    def _():
        total = l_ref[:, 0:1]
        out = (acc_ref[...] / total).astype(BF16)
        lse = m_ref[:, 0:1] * scale + jnp.log2(total)
        lse_ref[head] = jnp.broadcast_to(lse, lse_ref.shape[1:])
        for c in range(sources):
            o_ref[c, pl.ds(head * rows, rows), :] = out[c * rows : (c + 1) * rows]

    @pl.when(jnp.logical_and(block == last, head == heads - 1))
    def _():
        for c in range(sources):
            column = jnp.concatenate(
                [lse_ref[h, c * rows : (c + 1) * rows, :] for h in range(heads)], axis=0
            )
            row = column.T[0:8]
            high = row.astype(BF16).astype(F32)
            middle = (row - high).astype(BF16).astype(F32)
            low = row - high - middle
            place = lax.broadcasted_iota(jnp.int32, row.shape, 0)
            stats = jnp.where(place == 0, high, jnp.where(place == 1, middle, low))
            o_ref[c, pl.ds(heads * rows, 8), :] = stats.astype(BF16)


def prefix_attention(q, keys, values, scale):
    sources, heads, rows, dim = q.shape
    length = keys.shape[1]
    block = 1024 if length % 1024 == 0 else length
    total_rows = sources * rows
    return pl.pallas_call(
        functools.partial(prefix_kernel, scale),
        grid=(heads, length // block),
        in_specs=[
            pl.BlockSpec(q.shape, lambda h, b: (0, 0, 0, 0)),
            pl.BlockSpec((1, block, dim), lambda h, b: (h, b, 0)),
            pl.BlockSpec((1, block, dim), lambda h, b: (h, b, 0)),
        ],
        out_specs=pl.BlockSpec((sources, heads * rows + 8, dim), lambda h, b: (0, 0, 0)),
        out_shape=jax.ShapeDtypeStruct((sources, heads * rows + 8, dim), BF16),
        scratch_shapes=[
            pltpu.VMEM((total_rows, 128), F32),
            pltpu.VMEM((total_rows, 128), F32),
            pltpu.VMEM((total_rows, dim), F32),
            pltpu.VMEM((heads, total_rows, 128), F32),
        ],
        compiler_params=pltpu.CompilerParams(
            dimension_semantics=("arbitrary", "arbitrary"), vmem_limit_bytes=32 << 20
        ),
        cost_estimate=pl.CostEstimate(
            flops=4 * heads * total_rows * length * dim,
            bytes_accessed=4 * heads * length * dim,
            transcendentals=heads * total_rows * length,
        ),
        name="prefix_attention",
    )(q, keys, values)


def suffix_kernel(scale, lengths_ref, q_ref, k_ref, v_ref, o_ref, lse_ref):
    session = pl.program_id(0)
    heads, length = k_ref.shape[1], k_ref.shape[2]
    group = q_ref.shape[1] // heads
    sessions = pl.num_programs(0)
    live = lengths_ref[session]
    for h in range(heads):
        q = q_ref[0, h * group : (h + 1) * group]
        scores = lax.dot_general(q, k_ref[0, h], NT, preferred_element_type=F32)
        position = lax.broadcasted_iota(jnp.int32, scores.shape, 1)
        scores = jnp.where(position < live, scores, -1e30)
        top = jnp.max(scores, axis=1, keepdims=True)
        weights = jnp.exp2((scores - top) * scale)
        total = jnp.sum(weights, axis=1, keepdims=True)
        out = jnp.dot(weights.astype(BF16), v_ref[0, h], preferred_element_type=F32) / total
        rows = pl.ds(h * group * o_ref.shape[0] // (heads * group) + session, group, stride=8)
        o_ref[rows, :] = out
        lse_ref[rows, :] = jnp.broadcast_to(top * scale + jnp.log2(total), out.shape)


def suffix_attention(q, keys, values, lengths, scale):
    sessions, heads, length, dim = keys.shape
    rows = q.shape[1] * sessions
    spec = pl.BlockSpec((rows, dim), lambda s, n: (0, 0))
    return pl.pallas_call(
        functools.partial(suffix_kernel, scale),
        grid_spec=pltpu.PrefetchScalarGridSpec(
            num_scalar_prefetch=1,
            grid=(sessions,),
            in_specs=[
                pl.BlockSpec((1,) + q.shape[1:], lambda s, n: (s, 0, 0)),
                pl.BlockSpec((1, heads, length, dim), lambda s, n: (s, 0, 0, 0)),
                pl.BlockSpec((1, heads, length, dim), lambda s, n: (s, 0, 0, 0)),
            ],
            out_specs=[spec, spec],
        ),
        out_shape=[jax.ShapeDtypeStruct((rows, dim), F32)] * 2,
        compiler_params=pltpu.CompilerParams(vmem_limit_bytes=16 << 20),
        cost_estimate=pl.CostEstimate(
            flops=4 * rows * length * dim,
            bytes_accessed=4 * sessions * heads * length * dim,
            transcendentals=rows * length,
        ),
        name="suffix_attention",
    )(lengths, q, keys, values)


def merge_kernel(parts_ref, suffix_ref, suffix_lse_ref, out_ref):
    sources, padded, dim = parts_ref.shape
    rows = padded - 8
    sessions = out_ref.shape[0]
    stats = []
    for c in range(sources):
        three = parts_ref[c, rows : rows + 8, :].astype(F32)
        stats.append(three[0:1] + three[1:2] + three[2:3])
    filler = jnp.full((rows - sources, rows), -3e38, F32)
    table = jnp.concatenate(stats + [filler], axis=0).T
    own = suffix_lse_ref[...]
    top = jnp.maximum(jnp.max(table, axis=1, keepdims=True), own[:, 0:1])
    shares = jnp.exp2(table - top)
    own_share = jnp.exp2(own[:, 0:1] - top)
    total = jnp.sum(shares, axis=1, keepdims=True) + own_share
    result = own_share * suffix_ref[...]
    for c in range(sources):
        result += shares[:, c : c + 1] * parts_ref[c, 0:rows, :].astype(F32)
    result = result / total
    for h in range(rows // sessions):
        out_ref[:, h * dim : (h + 1) * dim] = result[h * sessions : (h + 1) * sessions].astype(BF16)


def merge(parts, suffix, suffix_lse, sessions):
    rows, dim = suffix.shape
    return pl.pallas_call(
        merge_kernel,
        out_shape=jax.ShapeDtypeStruct((sessions, rows // sessions * dim), BF16),
        name="merge_shards",
    )(parts, suffix, suffix_lse)


def project_kernel(attended_ref, *refs):
    weights, out_ref = refs[:-1], refs[-1]
    heads, _, rows, _ = out_ref.shape
    for x, weight_ref in enumerate(weights):
        product = jnp.dot(attended_ref[...], weight_ref[...], preferred_element_type=F32)
        for h in range(heads):
            out_ref[h, x] = product[h * rows : (h + 1) * rows].astype(BF16)


def project(attended, weights, heads):
    sessions, features = attended.shape
    columns = weights[0].shape[1]
    return pl.pallas_call(
        project_kernel,
        out_shape=jax.ShapeDtypeStruct((heads, len(weights), sessions // heads, columns), BF16),
        compiler_params=pltpu.CompilerParams(vmem_limit_bytes=32 << 20),
        name="project",
    )(attended, *weights)


def finish_kernel(parts_ref, out_ref):
    for x in range(parts_ref.shape[1]):
        total = parts_ref[0, x].astype(F32)
        for h in range(1, parts_ref.shape[0]):
            total += parts_ref[h, x].astype(F32)
        out_ref[:, x] = total


def finish(parts):
    _, x, outer, sessions, columns = parts.shape
    return pl.pallas_call(
        finish_kernel,
        out_shape=jax.ShapeDtypeStruct((outer, x, sessions, columns), F32),
        name="sum_heads",
    )(parts)


def per_device(queries, prefix_keys, prefix_values, suffix_keys, suffix_values, lengths, out_weight):
    sessions, local_heads, dim = queries.shape
    kv_local = prefix_keys.shape[0]
    rows = local_heads // kv_local * sessions
    scale = LOG2E / math.sqrt(dim)
    ctx = lax.axis_size("ctx")
    heads = lax.axis_size("yh") * lax.axis_size("core")
    wide = lax.axis_size("x")
    low = lax.axis_size("yl")

    arranged = queries.transpose(1, 0, 2).reshape(1, kv_local, rows, dim)
    spread = jnp.broadcast_to(arranged, (ctx, kv_local, rows, dim))
    gathered = lax.all_to_all(spread, "ctx", 0, 0, tiled=True)
    weight_spread = jnp.broadcast_to(out_weight[None], (wide,) + out_weight.shape)
    weight_all = lax.all_to_all(weight_spread, "x", 0, 0, tiled=True)

    suffix, suffix_lse = suffix_attention(queries, suffix_keys, suffix_values, lengths, scale)
    parts = prefix_attention(gathered, prefix_keys, prefix_values, scale)
    parts = lax.all_to_all(parts, "ctx", 0, 0, tiled=True)
    attended = merge(parts, suffix, suffix_lse, sessions)

    group = ctx * low
    everyone = jnp.broadcast_to(attended[None], (group,) + attended.shape)
    everyone = lax.all_to_all(everyone, ("ctx", "yl"), 0, 0, tiled=True)
    everyone = everyone.reshape(group * sessions, attended.shape[1])
    partial_out = project(everyone, [weight_all[x] for x in range(wide)], heads)
    partial_out = partial_out.reshape(heads * wide, group * sessions // heads, out_weight.shape[1])
    partial_out = lax.all_to_all(partial_out, ("yh", "core", "x"), 0, 0, tiled=True)
    partial_out = partial_out.reshape(heads, wide, group // heads, sessions, out_weight.shape[1])
    return finish(partial_out).reshape(group * sessions * wide // heads, out_weight.shape[1])


def solution(mesh):
    fine = Mesh(mesh.devices.reshape(8, 2, 2, 2, 4), ("ctx", "yh", "core", "yl", "x"))
    both = ("ctx",) + SESS
    return jax.shard_map(
        per_device,
        mesh=fine,
        in_specs=(
            P(both, HEAD, None),
            P(HEAD, "ctx", None),
            P(HEAD, "ctx", None),
            P(both, HEAD, None, None),
            P(both, HEAD, None, None),
            P(both),
            P(HEAD, both),
        ),
        out_specs=P(HEAD, both),
        check_vma=False,
    )
```

```python
import functools
import math

import jax
import jax.numpy as jnp
from jax import lax
from jax.experimental import pallas as pl
from jax.experimental.pallas import tpu as pltpu
from jax.sharding import Mesh
from jax.sharding import PartitionSpec as P

F32 = jnp.float32
BF16 = jnp.bfloat16
LOG2E = 1.4426950408889634
HEAD = ("yh", "core")
SESS = ("yl", "x")
NT = (((1,), (1,)), ((), ()))


def prefix_kernel(
    scale, chunk, block, q_ref, k_hbm, v_hbm, o_ref, k_ref, v_ref, acc_ref, lse_ref, k_sem, v_sem
):
    head = pl.program_id(0)
    sources, _, rows, dim = q_ref.shape
    heads, length, _ = k_ref.shape
    tiles = [(c, k) for c in range(0, sources, chunk) for k in range(0, length, block)]

    def copy_of(source, target, sem, h, part):
        span = pl.ds(part * block, block)
        return pltpu.make_async_copy(source.at[h, span], target.at[h, span], sem.at[h, part])

    @pl.when(head == 0)
    def _():
        for h in range(heads):
            for part in range(length // block):
                copy_of(k_hbm, k_ref, k_sem, h, part).start()
                copy_of(v_hbm, v_ref, v_sem, h, part).start()

    def scores_of(tile):
        c, k = tile
        q = q_ref[c : c + chunk, 0].reshape(chunk * rows, dim)
        if c == 0:
            copy_of(k_hbm, k_ref, k_sem, head, k // block).wait()
        return lax.dot_general(q, k_ref[head, k : k + block], NT, preferred_element_type=F32)

    scores = scores_of(tiles[0])
    for index, (c, k) in enumerate(tiles):
        if c == 0:
            copy_of(v_hbm, v_ref, v_sem, head, k // block).wait()
        ahead = scores_of(tiles[index + 1]) if index + 1 < len(tiles) else None
        new = jnp.max(scores, axis=1, keepdims=True)
        if k > 0:
            new = jnp.maximum(top, new)
            factor = jnp.exp2((top - new) * scale)
        weights = jnp.exp2((scores - new) * scale)
        part = jnp.sum(weights, axis=1, keepdims=True)
        product = jnp.dot(
            weights.astype(BF16), v_ref[head, k : k + block], preferred_element_type=F32
        )
        span = slice(c * rows, (c + chunk) * rows)
        if k > 0:
            total = total * factor + part
            product = acc_ref[span] * factor + product
        else:
            total = part
        top, scores = new, ahead
        if k + block < length:
            acc_ref[span] = product
            continue
        out = (product / total).astype(BF16)
        lse = top * scale + jnp.log2(total)
        lse_ref[head, span] = jnp.broadcast_to(lse, (chunk * rows, lse_ref.shape[2]))
        for i in range(chunk):
            o_ref[c + i, pl.ds(head * rows, rows), :] = out[i * rows : (i + 1) * rows]

    @pl.when(head == heads - 1)
    def _():
        for c in range(sources):
            column = jnp.concatenate(
                [lse_ref[h, c * rows : (c + 1) * rows, :] for h in range(heads)], axis=0
            )
            row = column.T[0:8]
            high = row.astype(BF16).astype(F32)
            middle = (row - high).astype(BF16).astype(F32)
            low = row - high - middle
            place = lax.broadcasted_iota(jnp.int32, row.shape, 0)
            stats = jnp.where(place == 0, high, jnp.where(place == 1, middle, low))
            o_ref[c, pl.ds(heads * rows, 8), :] = stats.astype(BF16)


def prefix_attention(q, keys, values, scale):
    sources, heads, rows, dim = q.shape
    length = keys.shape[1]
    block = length // 2
    total_rows = sources * rows
    return pl.pallas_call(
        functools.partial(prefix_kernel, scale, 2, block),
        grid=(heads,),
        in_specs=[
            pl.BlockSpec((sources, 1, rows, dim), lambda h: (0, h, 0, 0)),
            pl.BlockSpec(memory_space=pl.ANY),
            pl.BlockSpec(memory_space=pl.ANY),
        ],
        out_specs=pl.BlockSpec((sources, heads * rows + 8, dim), lambda h: (0, 0, 0)),
        out_shape=jax.ShapeDtypeStruct((sources, heads * rows + 8, dim), BF16),
        scratch_shapes=[
            pltpu.VMEM(keys.shape, BF16),
            pltpu.VMEM(values.shape, BF16),
            pltpu.VMEM((total_rows, dim), F32),
            pltpu.VMEM((heads, total_rows, 128), F32),
            pltpu.SemaphoreType.DMA((heads, length // block)),
            pltpu.SemaphoreType.DMA((heads, length // block)),
        ],
        compiler_params=pltpu.CompilerParams(
            dimension_semantics=("arbitrary",), vmem_limit_bytes=58 << 20
        ),
        cost_estimate=pl.CostEstimate(
            flops=4 * heads * total_rows * length * dim,
            bytes_accessed=4 * heads * length * dim,
            transcendentals=heads * total_rows * length,
        ),
        name="prefix_attention",
    )(q, keys, values)


def suffix_kernel(scale, lengths_ref, q_ref, k_ref, v_ref, o_ref, lse_ref):
    step = pl.program_id(0)
    count, heads, length = k_ref.shape[0], k_ref.shape[1], k_ref.shape[2]
    group = q_ref.shape[1] // heads
    sessions = pl.num_programs(0) * count
    pairs = [(s, h) for s in range(count) for h in range(heads)]
    all_scores = [
        lax.dot_general(
            q_ref[s, h * group : (h + 1) * group], k_ref[s, h], NT, preferred_element_type=F32
        )
        for s, h in pairs
    ]
    position = lax.broadcasted_iota(jnp.int32, (group, length), 1)
    softened = []
    for (s, h), scores in zip(pairs, all_scores):
        scores = jnp.where(position < lengths_ref[step * count + s], scores, -1e30)
        top = jnp.max(scores, axis=1, keepdims=True)
        weights = jnp.exp2((scores - top) * scale)
        softened.append((top, jnp.sum(weights, axis=1, keepdims=True), weights.astype(BF16)))
    for (s, h), (top, total, weights) in zip(pairs, softened):
        out = jnp.dot(weights, v_ref[s, h], preferred_element_type=F32) / total
        rows = pl.ds(h * group * sessions + step * count + s, group, stride=sessions)
        o_ref[rows, :] = out
        lse_ref[rows, :] = jnp.broadcast_to(top * scale + jnp.log2(total), out.shape)


def suffix_attention(q, keys, values, lengths, scale):
    sessions, heads, length, dim = keys.shape
    rows = q.shape[1] * sessions
    count = 4
    spec = pl.BlockSpec((rows, dim), lambda s, n: (0, 0))
    return pl.pallas_call(
        functools.partial(suffix_kernel, scale),
        grid_spec=pltpu.PrefetchScalarGridSpec(
            num_scalar_prefetch=1,
            grid=(sessions // count,),
            in_specs=[
                pl.BlockSpec((count,) + q.shape[1:], lambda s, n: (s, 0, 0)),
                pl.BlockSpec((count, heads, length, dim), lambda s, n: (s, 0, 0, 0)),
                pl.BlockSpec((count, heads, length, dim), lambda s, n: (s, 0, 0, 0)),
            ],
            out_specs=[spec, spec],
        ),
        out_shape=[jax.ShapeDtypeStruct((rows, dim), F32)] * 2,
        compiler_params=pltpu.CompilerParams(vmem_limit_bytes=56 << 20),
        cost_estimate=pl.CostEstimate(
            flops=4 * rows * length * dim,
            bytes_accessed=4 * sessions * heads * length * dim,
            transcendentals=rows * length,
        ),
        name="suffix_attention",
    )(lengths, q, keys, values)


def merge_kernel(parts_ref, suffix_ref, suffix_lse_ref, out_ref):
    sources, padded, dim = parts_ref.shape
    rows = padded - 8
    copies, sessions, _ = out_ref.shape
    stats = []
    for c in range(sources):
        three = parts_ref[c, rows : rows + 8, :].astype(F32)
        stats.append(three[0:1] + three[1:2] + three[2:3])
    filler = jnp.full((rows - sources, rows), -3e38, F32)
    table = jnp.concatenate(stats + [filler], axis=0).T
    own = suffix_lse_ref[...]
    top = jnp.maximum(jnp.max(table, axis=1, keepdims=True), own[:, 0:1])
    shares = jnp.exp2(table - top)
    own_share = jnp.exp2(own[:, 0:1] - top)
    total = jnp.sum(shares, axis=1, keepdims=True) + own_share
    result = own_share * suffix_ref[...]
    for c in range(sources):
        result += shares[:, c : c + 1] * parts_ref[c, 0:rows, :].astype(F32)
    result = result / total
    for h in range(rows // sessions):
        piece = result[h * sessions : (h + 1) * sessions].astype(BF16)
        for copy in range(copies):
            out_ref[copy, :, h * dim : (h + 1) * dim] = piece


def merge(parts, suffix, suffix_lse, sessions, copies):
    rows, dim = suffix.shape
    return pl.pallas_call(
        merge_kernel,
        out_shape=jax.ShapeDtypeStruct((copies, sessions, rows // sessions * dim), BF16),
        name="merge_shards",
    )(parts, suffix, suffix_lse)


def project_kernel(attended_ref, weight_ref, out_ref):
    product = jnp.dot(attended_ref[...], weight_ref[0], preferred_element_type=F32)
    heads, _, rows, _ = out_ref.shape
    for h in range(heads):
        out_ref[h, 0] = product[h * rows : (h + 1) * rows].astype(BF16)


def project(attended, weights, heads):
    sessions, features = attended.shape
    wide, _, columns = weights.shape
    rows = sessions // heads
    return pl.pallas_call(
        project_kernel,
        grid=(wide,),
        in_specs=[
            pl.BlockSpec((sessions, features), lambda x: (0, 0)),
            pl.BlockSpec((1, features, columns), lambda x: (x, 0, 0)),
        ],
        out_specs=pl.BlockSpec((heads, 1, rows, columns), lambda x: (0, x, 0, 0)),
        out_shape=jax.ShapeDtypeStruct((heads, wide, rows, columns), BF16),
        compiler_params=pltpu.CompilerParams(vmem_limit_bytes=16 << 20),
        name="project",
    )(attended, weights)


def finish_kernel(parts_ref, out_ref):
    for x in range(parts_ref.shape[1]):
        total = parts_ref[0, x].astype(F32)
        for h in range(1, parts_ref.shape[0]):
            total += parts_ref[h, x].astype(F32)
        out_ref[:, x] = total


def finish(parts):
    _, x, outer, sessions, columns = parts.shape
    return pl.pallas_call(
        finish_kernel,
        out_shape=jax.ShapeDtypeStruct((outer, x, sessions, columns), F32),
        name="sum_heads",
    )(parts)


def per_device(queries, prefix_keys, prefix_values, suffix_keys, suffix_values, lengths, out_weight):
    sessions, local_heads, dim = queries.shape
    kv_local = prefix_keys.shape[0]
    rows = local_heads // kv_local * sessions
    scale = LOG2E / math.sqrt(dim)
    ctx = lax.axis_size("ctx")
    heads = lax.axis_size("yh") * lax.axis_size("core")
    wide = lax.axis_size("x")
    low = lax.axis_size("yl")

    arranged = queries.transpose(1, 0, 2).reshape(1, kv_local, rows, dim)
    spread = jnp.broadcast_to(arranged, (ctx, kv_local, rows, dim))
    gathered = lax.all_to_all(spread, "ctx", 0, 0, tiled=True)
    weight_all = lax.all_gather(out_weight, "x", axis=0)

    suffix, suffix_lse = suffix_attention(queries, suffix_keys, suffix_values, lengths, scale)
    gathered, suffix, suffix_lse = lax.optimization_barrier((gathered, suffix, suffix_lse))
    parts = prefix_attention(gathered, prefix_keys, prefix_values, scale)
    parts = lax.all_to_all(parts, "ctx", 0, 0, tiled=True)

    group = ctx * low
    everyone = merge(parts, suffix, suffix_lse, sessions, group)
    everyone, weight_all = lax.optimization_barrier((everyone, weight_all))
    everyone = lax.all_to_all(everyone, ("ctx", "yl"), 0, 0, tiled=True)
    everyone = everyone.reshape(group * sessions, local_heads * dim)
    partial_out = project(everyone, weight_all, heads)
    partial_out = partial_out.reshape(heads * wide, group * sessions // heads, out_weight.shape[1])
    partial_out = lax.all_to_all(partial_out, ("yh", "core", "x"), 0, 0, tiled=True)
    partial_out = partial_out.reshape(heads, wide, group // heads, sessions, out_weight.shape[1])
    return finish(partial_out).reshape(group * sessions * wide // heads, out_weight.shape[1])


def solution(mesh):
    fine = Mesh(mesh.devices.reshape(8, 2, 2, 2, 4), ("ctx", "yh", "core", "yl", "x"))
    both = ("ctx",) + SESS
    return jax.shard_map(
        per_device,
        mesh=fine,
        in_specs=(
            P(both, HEAD, None),
            P(HEAD, "ctx", None),
            P(HEAD, "ctx", None),
            P(both, HEAD, None, None),
            P(both, HEAD, None, None),
            P(both),
            P(HEAD, both),
        ),
        out_specs=P(HEAD, both),
        check_vma=False,
    )
```

```python
import functools
import math

import jax
import jax.numpy as jnp
from jax import lax
from jax.experimental import pallas as pl
from jax.experimental.pallas import tpu as pltpu
from jax.sharding import Mesh
from jax.sharding import PartitionSpec as P

F32 = jnp.float32
BF16 = jnp.bfloat16
LOG2E = 1.4426950408889634
HEAD = ("yh", "core")
SESS = ("yl", "x")
NT = (((1,), (1,)), ((), ()))


def prefix_kernel(
    scale, chunk, block, q_ref, k_hbm, v_hbm, o_ref, k_ref, v_ref, acc_ref, lse_ref, k_sem, v_sem
):
    head = pl.program_id(0)
    sources, _, rows, dim = q_ref.shape
    heads, length, _ = k_ref.shape
    tiles = [(c, k) for c in range(0, sources, chunk) for k in range(0, length, block)]

    def copy_of(source, target, sem, h, part):
        span = pl.ds(part * block, block)
        return pltpu.make_async_copy(source.at[h, span], target.at[h, span], sem.at[h, part])

    @pl.when(head == 0)
    def _():
        for h in range(heads):
            for part in range(length // block):
                copy_of(k_hbm, k_ref, k_sem, h, part).start()
                copy_of(v_hbm, v_ref, v_sem, h, part).start()

    def scores_of(tile):
        c, k = tile
        q = q_ref[c : c + chunk, 0].reshape(chunk * rows, dim)
        if c == 0:
            copy_of(k_hbm, k_ref, k_sem, head, k // block).wait()
        return lax.dot_general(q, k_ref[head, k : k + block], NT, preferred_element_type=F32)

    scores = scores_of(tiles[0])
    for index, (c, k) in enumerate(tiles):
        if c == 0:
            copy_of(v_hbm, v_ref, v_sem, head, k // block).wait()
        ahead = scores_of(tiles[index + 1]) if index + 1 < len(tiles) else None
        new = jnp.max(scores, axis=1, keepdims=True)
        if k > 0:
            new = jnp.maximum(top, new)
            factor = jnp.exp2((top - new) * scale)
        weights = jnp.exp2((scores - new) * scale)
        part = jnp.sum(weights, axis=1, keepdims=True)
        product = jnp.dot(
            weights.astype(BF16), v_ref[head, k : k + block], preferred_element_type=F32
        )
        span = slice(c * rows, (c + chunk) * rows)
        if k > 0:
            total = total * factor + part
            product = acc_ref[span] * factor + product
        else:
            total = part
        top, scores = new, ahead
        if k + block < length:
            acc_ref[span] = product
            continue
        out = (product / total).astype(BF16)
        lse = top * scale + jnp.log2(total)
        lse_ref[head, span] = jnp.broadcast_to(lse, (chunk * rows, lse_ref.shape[2]))
        for i in range(chunk):
            o_ref[c + i, pl.ds(head * rows, rows), :] = out[i * rows : (i + 1) * rows]

    @pl.when(head == heads - 1)
    def _():
        for c in range(sources):
            column = jnp.concatenate(
                [lse_ref[h, c * rows : (c + 1) * rows, :] for h in range(heads)], axis=0
            )
            row = column.T[0:8]
            high = row.astype(BF16).astype(F32)
            middle = (row - high).astype(BF16).astype(F32)
            low = row - high - middle
            place = lax.broadcasted_iota(jnp.int32, row.shape, 0)
            stats = jnp.where(place == 0, high, jnp.where(place == 1, middle, low))
            o_ref[c, pl.ds(heads * rows, 8), :] = stats.astype(BF16)


def prefix_attention(q, keys, values, scale):
    sources, heads, rows, dim = q.shape
    length = keys.shape[1]
    block = length // 2
    total_rows = sources * rows
    return pl.pallas_call(
        functools.partial(prefix_kernel, scale, 2, block),
        grid=(heads,),
        in_specs=[
            pl.BlockSpec((sources, 1, rows, dim), lambda h: (0, h, 0, 0)),
            pl.BlockSpec(memory_space=pltpu.HBM),
            pl.BlockSpec(memory_space=pltpu.HBM),
        ],
        out_specs=pl.BlockSpec((sources, heads * rows + 8, dim), lambda h: (0, 0, 0)),
        out_shape=jax.ShapeDtypeStruct((sources, heads * rows + 8, dim), BF16),
        scratch_shapes=[
            pltpu.VMEM(keys.shape, BF16),
            pltpu.VMEM(values.shape, BF16),
            pltpu.VMEM((total_rows, dim), F32),
            pltpu.VMEM((heads, total_rows, 128), F32),
            pltpu.SemaphoreType.DMA((heads, length // block)),
            pltpu.SemaphoreType.DMA((heads, length // block)),
        ],
        compiler_params=pltpu.CompilerParams(
            dimension_semantics=("arbitrary",), vmem_limit_bytes=32 << 20
        ),
        cost_estimate=pl.CostEstimate(
            flops=4 * heads * total_rows * length * dim,
            bytes_accessed=4 * heads * length * dim,
            transcendentals=heads * total_rows * length,
        ),
        name="prefix_attention",
    )(
        q,
        pltpu.with_memory_space_constraint(keys, pltpu.HBM),
        pltpu.with_memory_space_constraint(values, pltpu.HBM),
    )


def suffix_kernel(scale, lengths_ref, q_ref, k_ref, v_ref, o_ref, lse_ref):
    step = pl.program_id(0)
    count, heads, length = k_ref.shape[0], k_ref.shape[1], k_ref.shape[2]
    group = q_ref.shape[1] // heads
    sessions = pl.num_programs(0) * count
    pairs = [(s, h) for s in range(count) for h in range(heads)]
    all_scores = [
        lax.dot_general(
            q_ref[s, h * group : (h + 1) * group], k_ref[s, h], NT, preferred_element_type=F32
        )
        for s, h in pairs
    ]
    position = lax.broadcasted_iota(jnp.int32, (group, length), 1)
    softened = []
    for (s, h), scores in zip(pairs, all_scores):
        scores = jnp.where(position < lengths_ref[step * count + s], scores, -1e30)
        top = jnp.max(scores, axis=1, keepdims=True)
        weights = jnp.exp2((scores - top) * scale)
        softened.append((top, jnp.sum(weights, axis=1, keepdims=True), weights.astype(BF16)))
    for (s, h), (top, total, weights) in zip(pairs, softened):
        out = jnp.dot(weights, v_ref[s, h], preferred_element_type=F32) / total
        rows = pl.ds(h * group * sessions + step * count + s, group, stride=sessions)
        o_ref[rows, :] = out
        lse_ref[rows, :] = jnp.broadcast_to(top * scale + jnp.log2(total), out.shape)


def suffix_attention(q, keys, values, lengths, scale):
    sessions, heads, length, dim = keys.shape
    rows = q.shape[1] * sessions
    count = 4
    spec = pl.BlockSpec((rows, dim), lambda s, n: (0, 0))
    return pl.pallas_call(
        functools.partial(suffix_kernel, scale),
        grid_spec=pltpu.PrefetchScalarGridSpec(
            num_scalar_prefetch=1,
            grid=(sessions // count,),
            in_specs=[
                pl.BlockSpec((count,) + q.shape[1:], lambda s, n: (s, 0, 0)),
                pl.BlockSpec((count, heads, length, dim), lambda s, n: (s, 0, 0, 0)),
                pl.BlockSpec((count, heads, length, dim), lambda s, n: (s, 0, 0, 0)),
            ],
            out_specs=[spec, spec],
        ),
        out_shape=[jax.ShapeDtypeStruct((rows, dim), F32)] * 2,
        compiler_params=pltpu.CompilerParams(vmem_limit_bytes=56 << 20),
        cost_estimate=pl.CostEstimate(
            flops=4 * rows * length * dim,
            bytes_accessed=4 * sessions * heads * length * dim,
            transcendentals=rows * length,
        ),
        name="suffix_attention",
    )(lengths, q, keys, values)


def merge_kernel(parts_ref, suffix_ref, suffix_lse_ref, out_ref):
    sources, padded, dim = parts_ref.shape
    rows = padded - 8
    copies, sessions, _ = out_ref.shape
    stats = []
    for c in range(sources):
        three = parts_ref[c, rows : rows + 8, :].astype(F32)
        stats.append(three[0:1] + three[1:2] + three[2:3])
    filler = jnp.full((rows - sources, rows), -3e38, F32)
    table = jnp.concatenate(stats + [filler], axis=0).T
    own = suffix_lse_ref[...]
    top = jnp.maximum(jnp.max(table, axis=1, keepdims=True), own[:, 0:1])
    shares = jnp.exp2(table - top)
    own_share = jnp.exp2(own[:, 0:1] - top)
    total = jnp.sum(shares, axis=1, keepdims=True) + own_share
    result = own_share * suffix_ref[...]
    for c in range(sources):
        result += shares[:, c : c + 1] * parts_ref[c, 0:rows, :].astype(F32)
    result = result / total
    for h in range(rows // sessions):
        piece = result[h * sessions : (h + 1) * sessions].astype(BF16)
        for copy in range(copies):
            out_ref[copy, :, h * dim : (h + 1) * dim] = piece


def merge(parts, suffix, suffix_lse, sessions, copies):
    rows, dim = suffix.shape
    return pl.pallas_call(
        merge_kernel,
        out_shape=jax.ShapeDtypeStruct((copies, sessions, rows // sessions * dim), BF16),
        name="merge_shards",
    )(parts, suffix, suffix_lse)


def project_kernel(place_ref, attended_ref, *refs):
    weights, out_ref = refs[:-1], refs[-1]
    heads, wide, rows, columns = out_ref.shape
    for k, weight_ref in enumerate(weights):
        product = jnp.dot(attended_ref[...], weight_ref[...], preferred_element_type=F32)
        x = lax.rem(place_ref[0] + (wide - k), wide)
        out_ref[:, x] = product.astype(BF16).reshape(heads, rows, columns)


def project(place, attended, weights, heads):
    sessions, features = attended.shape
    columns = weights[0].shape[1]
    vmem = pl.BlockSpec(memory_space=pltpu.VMEM)
    return pl.pallas_call(
        project_kernel,
        in_specs=[pl.BlockSpec(memory_space=pltpu.SMEM)] + [vmem] * (1 + len(weights)),
        out_specs=vmem,
        out_shape=jax.ShapeDtypeStruct((heads, len(weights), sessions // heads, columns), BF16),
        compiler_params=pltpu.CompilerParams(vmem_limit_bytes=16 << 20),
        name="project",
    )(place, attended, *weights)


def finish_kernel(parts_ref, out_ref):
    for x in range(parts_ref.shape[1]):
        total = parts_ref[0, x].astype(F32)
        for h in range(1, parts_ref.shape[0]):
            total += parts_ref[h, x].astype(F32)
        out_ref[:, x] = total


def finish(parts):
    _, x, outer, sessions, columns = parts.shape
    return pl.pallas_call(
        finish_kernel,
        out_shape=jax.ShapeDtypeStruct((outer, x, sessions, columns), F32),
        name="sum_heads",
    )(parts)


def per_device(queries, prefix_keys, prefix_values, suffix_keys, suffix_values, lengths, out_weight):
    sessions, local_heads, dim = queries.shape
    kv_local = prefix_keys.shape[0]
    rows = local_heads // kv_local * sessions
    scale = LOG2E / math.sqrt(dim)
    ctx = lax.axis_size("ctx")
    heads = lax.axis_size("yh") * lax.axis_size("core")
    wide = lax.axis_size("x")
    low = lax.axis_size("yl")

    arranged = queries.transpose(1, 0, 2).reshape(1, kv_local, rows, dim)
    spread = jnp.broadcast_to(arranged, (ctx, kv_local, rows, dim))
    gathered = lax.all_to_all(spread, "ctx", 0, 0, tiled=True)
    weights = [out_weight]
    for k in range(1, wide):
        pairs = [(x, (x + k) % wide) for x in range(wide)]
        weights.append(lax.ppermute(out_weight, "x", pairs))

    suffix, suffix_lse = suffix_attention(queries, suffix_keys, suffix_values, lengths, scale)
    gathered, suffix, suffix_lse = lax.optimization_barrier((gathered, suffix, suffix_lse))
    parts = prefix_attention(gathered, prefix_keys, prefix_values, scale)
    parts = lax.all_to_all(parts, "ctx", 0, 0, tiled=True)

    group = ctx * low
    everyone = merge(parts, suffix, suffix_lse, sessions, group)
    everyone, weights = lax.optimization_barrier((everyone, weights))
    everyone = lax.all_to_all(everyone, ("ctx", "yl"), 0, 0, tiled=True)
    everyone = everyone.reshape(group * sessions, local_heads * dim)
    place = lax.axis_index("x").astype(jnp.int32).reshape(1)
    partial_out = project(place, everyone, weights, heads)
    partial_out = partial_out.reshape(heads * wide, group * sessions // heads, out_weight.shape[1])
    partial_out = lax.all_to_all(partial_out, ("yh", "core", "x"), 0, 0, tiled=True)
    partial_out = partial_out.reshape(heads, wide, group // heads, sessions, out_weight.shape[1])
    return finish(partial_out).reshape(group * sessions * wide // heads, out_weight.shape[1])


def solution(mesh):
    fine = Mesh(mesh.devices.reshape(8, 2, 2, 2, 4), ("ctx", "yh", "core", "yl", "x"))
    both = ("ctx",) + SESS
    return jax.shard_map(
        per_device,
        mesh=fine,
        in_specs=(
            P(both, HEAD, None),
            P(HEAD, "ctx", None),
            P(HEAD, "ctx", None),
            P(both, HEAD, None, None),
            P(both, HEAD, None, None),
            P(both),
            P(HEAD, both),
        ),
        out_specs=P(HEAD, both),
        check_vma=False,
    )
```

```python
import functools
import math

import jax
import jax.numpy as jnp
from jax import lax
from jax.experimental import pallas as pl
from jax.experimental.pallas import tpu as pltpu
from jax.sharding import Mesh
from jax.sharding import PartitionSpec as P

F32 = jnp.float32
BF16 = jnp.bfloat16
LOG2E = 1.4426950408889634
HEAD = ("yh", "core")
SESS = ("yl", "x")
NT = (((1,), (1,)), ((), ()))


def prefix_kernel(
    scale, chunk, block, all_q_ref, k_hbm, v_hbm, o_ref, q_ref, k_ref, v_ref, acc_ref, lse_ref,
    k_sem, v_sem
):
    head = pl.program_id(0)
    sources, sessions, local_heads, dim = all_q_ref.shape
    heads, length, _ = k_ref.shape
    group = local_heads // heads
    rows = sessions * group
    tiles = [(c, k) for c in range(0, sources, chunk) for k in range(0, length, block)]

    def copy_of(source, target, sem, h, part):
        span = pl.ds(part * block, block)
        return pltpu.make_async_copy(source.at[h, span], target.at[h, span], sem.at[h, part])

    @pl.when(head == 0)
    def _():
        for h in range(heads):
            for part in range(length // block):
                copy_of(k_hbm, k_ref, k_sem, h, part).start()
                copy_of(v_hbm, v_ref, v_sem, h, part).start()
            part = all_q_ref[:, :, h * group : (h + 1) * group, :]
            q_ref[h] = part.reshape(sources * rows, dim)

    def scores_of(tile):
        c, k = tile
        q = q_ref[head, c * rows : (c + chunk) * rows]
        if c == 0:
            copy_of(k_hbm, k_ref, k_sem, head, k // block).wait()
        return lax.dot_general(q, k_ref[head, k : k + block], NT, preferred_element_type=F32)

    scores = scores_of(tiles[0])
    for index, (c, k) in enumerate(tiles):
        if c == 0:
            copy_of(v_hbm, v_ref, v_sem, head, k // block).wait()
        ahead = scores_of(tiles[index + 1]) if index + 1 < len(tiles) else None
        new = jnp.max(scores, axis=1, keepdims=True)
        if k > 0:
            new = jnp.maximum(top, new)
            factor = jnp.exp2((top - new) * scale)
        weights = jnp.exp2((scores - new) * scale)
        part = jnp.sum(weights, axis=1, keepdims=True)
        product = jnp.dot(
            weights.astype(BF16), v_ref[head, k : k + block], preferred_element_type=F32
        )
        span = slice(c * rows, (c + chunk) * rows)
        if k > 0:
            total = total * factor + part
            product = acc_ref[span] * factor + product
        else:
            total = part
        top, scores = new, ahead
        if k + block < length:
            acc_ref[span] = product
            continue
        out = (product / total).astype(BF16)
        lse = top * scale + jnp.log2(total)
        lse_ref[head, span] = jnp.broadcast_to(lse, (chunk * rows, lse_ref.shape[2]))
        for i in range(chunk):
            o_ref[c + i, pl.ds(head * rows, rows), :] = out[i * rows : (i + 1) * rows]

    @pl.when(head == heads - 1)
    def _():
        for c in range(sources):
            column = jnp.concatenate(
                [lse_ref[h, c * rows : (c + 1) * rows, :] for h in range(heads)], axis=0
            )
            row = column.T[0:8]
            high = row.astype(BF16).astype(F32)
            middle = (row - high).astype(BF16).astype(F32)
            low = row - high - middle
            place = lax.broadcasted_iota(jnp.int32, row.shape, 0)
            stats = jnp.where(place == 0, high, jnp.where(place == 1, middle, low))
            o_ref[c, pl.ds(heads * rows, 8), :] = stats.astype(BF16)


def prefix_attention(q, keys, values, scale):
    sources, sessions, local_heads, dim = q.shape
    heads, length, _ = keys.shape
    rows = sessions * local_heads // heads
    block = length // 2
    total_rows = sources * rows
    return pl.pallas_call(
        functools.partial(prefix_kernel, scale, 2, block),
        grid=(heads,),
        in_specs=[
            pl.BlockSpec(q.shape, lambda h: (0, 0, 0, 0)),
            pl.BlockSpec(memory_space=pltpu.HBM),
            pl.BlockSpec(memory_space=pltpu.HBM),
        ],
        out_specs=pl.BlockSpec((sources, heads * rows + 8, dim), lambda h: (0, 0, 0)),
        out_shape=jax.ShapeDtypeStruct((sources, heads * rows + 8, dim), BF16),
        scratch_shapes=[
            pltpu.VMEM((heads, total_rows, dim), BF16),
            pltpu.VMEM(keys.shape, BF16),
            pltpu.VMEM(values.shape, BF16),
            pltpu.VMEM((total_rows, dim), F32),
            pltpu.VMEM((heads, total_rows, 128), F32),
            pltpu.SemaphoreType.DMA((heads, length // block)),
            pltpu.SemaphoreType.DMA((heads, length // block)),
        ],
        compiler_params=pltpu.CompilerParams(
            dimension_semantics=("arbitrary",), vmem_limit_bytes=32 << 20
        ),
        cost_estimate=pl.CostEstimate(
            flops=4 * heads * total_rows * length * dim,
            bytes_accessed=4 * heads * length * dim,
            transcendentals=heads * total_rows * length,
        ),
        name="prefix_attention",
    )(
        q,
        pltpu.with_memory_space_constraint(keys, pltpu.HBM),
        pltpu.with_memory_space_constraint(values, pltpu.HBM),
    )


def suffix_kernel(scale, lengths_ref, q_ref, k_ref, v_ref, o_ref, lse_ref):
    step = pl.program_id(0)
    count, heads, length = k_ref.shape[0], k_ref.shape[1], k_ref.shape[2]
    group = q_ref.shape[1] // heads
    sessions = pl.num_programs(0) * count
    pairs = [(s, h) for s in range(count) for h in range(heads)]
    all_scores = [
        lax.dot_general(
            q_ref[s, h * group : (h + 1) * group], k_ref[s, h], NT, preferred_element_type=F32
        )
        for s, h in pairs
    ]
    position = lax.broadcasted_iota(jnp.int32, (group, length), 1)
    softened = []
    for (s, h), scores in zip(pairs, all_scores):
        scores = jnp.where(position < lengths_ref[step * count + s], scores, -1e30)
        top = jnp.max(scores, axis=1, keepdims=True)
        weights = jnp.exp2((scores - top) * scale)
        softened.append((top, jnp.sum(weights, axis=1, keepdims=True), weights.astype(BF16)))
    for (s, h), (top, total, weights) in zip(pairs, softened):
        out = jnp.dot(weights, v_ref[s, h], preferred_element_type=F32) / total
        rows = pl.ds((h * sessions + step * count + s) * group, group)
        o_ref[rows, :] = out
        lse_ref[rows, :] = jnp.broadcast_to(top * scale + jnp.log2(total), out.shape)


def suffix_attention(q, keys, values, lengths, scale):
    sessions, heads, length, dim = keys.shape
    rows = q.shape[1] * sessions
    count = 4
    spec = pl.BlockSpec((rows, dim), lambda s, n: (0, 0))
    return pl.pallas_call(
        functools.partial(suffix_kernel, scale),
        grid_spec=pltpu.PrefetchScalarGridSpec(
            num_scalar_prefetch=1,
            grid=(sessions // count,),
            in_specs=[
                pl.BlockSpec((count,) + q.shape[1:], lambda s, n: (s, 0, 0)),
                pl.BlockSpec((count, heads, length, dim), lambda s, n: (s, 0, 0, 0)),
                pl.BlockSpec((count, heads, length, dim), lambda s, n: (s, 0, 0, 0)),
            ],
            out_specs=[spec, spec],
        ),
        out_shape=[jax.ShapeDtypeStruct((rows, dim), F32)] * 2,
        compiler_params=pltpu.CompilerParams(vmem_limit_bytes=16 << 20),
        cost_estimate=pl.CostEstimate(
            flops=4 * rows * length * dim,
            bytes_accessed=4 * sessions * heads * length * dim,
            transcendentals=rows * length,
        ),
        name="suffix_attention",
    )(
        lengths,
        q,
        pltpu.with_memory_space_constraint(keys, pltpu.HBM),
        pltpu.with_memory_space_constraint(values, pltpu.HBM),
    )


def merge_kernel(heads, parts_ref, suffix_ref, suffix_lse_ref, out_ref, result_ref):
    sources, padded, dim = parts_ref.shape
    rows = padded - 8
    copies, sessions, _ = out_ref.shape
    stats = []
    for c in range(sources):
        three = parts_ref[c, rows : rows + 8, :].astype(F32)
        stats.append(three[0:1] + three[1:2] + three[2:3])
    filler = jnp.full((rows - sources, rows), -3e38, F32)
    table = jnp.concatenate(stats + [filler], axis=0).T
    own = suffix_lse_ref[...]
    top = jnp.maximum(jnp.max(table, axis=1, keepdims=True), own[:, 0:1])
    shares = jnp.exp2(table - top)
    own_share = jnp.exp2(own[:, 0:1] - top)
    total = jnp.sum(shares, axis=1, keepdims=True) + own_share
    result = own_share * suffix_ref[...]
    for c in range(sources):
        result += shares[:, c : c + 1] * parts_ref[c, 0:rows, :].astype(F32)
    result_ref[...] = result / total
    group = rows // sessions // heads
    for h in range(heads):
        for g in range(group):
            first = h * sessions * group + g
            piece = result_ref[pl.ds(first, sessions, stride=group), :].astype(BF16)
            column = (h * group + g) * dim
            for copy in range(copies):
                out_ref[copy, :, column : column + dim] = piece


def merge(parts, suffix, suffix_lse, sessions, heads, copies):
    rows, dim = suffix.shape
    return pl.pallas_call(
        functools.partial(merge_kernel, heads),
        scratch_shapes=[pltpu.VMEM((rows, dim), F32)],
        compiler_params=pltpu.CompilerParams(vmem_limit_bytes=16 << 20),
        out_shape=jax.ShapeDtypeStruct((copies, sessions, rows // sessions * dim), BF16),
        name="merge_shards",
    )(parts, suffix, suffix_lse)


def project_kernel(place_ref, attended_ref, *refs):
    weights, out_ref = refs[:-1], refs[-1]
    heads, wide, rows, columns = out_ref.shape
    for k, weight_ref in enumerate(weights):
        product = jnp.dot(attended_ref[...], weight_ref[...], preferred_element_type=F32)
        x = lax.rem(place_ref[0] + (wide - k), wide)
        out_ref[:, x] = product.astype(BF16).reshape(heads, rows, columns)


def project(place, attended, weights, heads):
    sessions, features = attended.shape
    columns = weights[0].shape[1]
    vmem = pl.BlockSpec(memory_space=pltpu.VMEM)
    return pl.pallas_call(
        project_kernel,
        in_specs=[pl.BlockSpec(memory_space=pltpu.SMEM)] + [vmem] * (1 + len(weights)),
        out_specs=vmem,
        out_shape=jax.ShapeDtypeStruct((heads, len(weights), sessions // heads, columns), BF16),
        compiler_params=pltpu.CompilerParams(vmem_limit_bytes=16 << 20),
        name="project",
    )(place, attended, *weights)


def finish_kernel(parts_ref, out_ref):
    for x in range(parts_ref.shape[1]):
        total = parts_ref[0, x].astype(F32)
        for h in range(1, parts_ref.shape[0]):
            total += parts_ref[h, x].astype(F32)
        out_ref[:, x] = total


def finish(parts):
    _, x, outer, sessions, columns = parts.shape
    return pl.pallas_call(
        finish_kernel,
        out_shape=jax.ShapeDtypeStruct((outer, x, sessions, columns), F32),
        compiler_params=pltpu.CompilerParams(vmem_limit_bytes=16 << 20),
        name="sum_heads",
    )(parts)


def per_device(queries, prefix_keys, prefix_values, suffix_keys, suffix_values, lengths, out_weight):
    sessions, local_heads, dim = queries.shape
    kv_local = prefix_keys.shape[0]
    scale = LOG2E / math.sqrt(dim)
    ctx = lax.axis_size("ctx")
    heads = lax.axis_size("yh") * lax.axis_size("core")
    wide = lax.axis_size("x")
    low = lax.axis_size("yl")

    spread = jnp.broadcast_to(queries[None], (ctx,) + queries.shape)
    gathered = lax.all_to_all(spread, "ctx", 0, 0, tiled=False)
    weights = [out_weight]
    for k in range(1, wide):
        pairs = [(x, (x + k) % wide) for x in range(wide)]
        weights.append(lax.ppermute(out_weight, "x", pairs))

    parts = prefix_attention(gathered, prefix_keys, prefix_values, scale)
    place = lax.axis_index("x").astype(jnp.int32).reshape(1)
    parts, queries, place = lax.optimization_barrier((parts, queries, place))
    parts = lax.all_to_all(parts, "ctx", 0, 0, tiled=True)
    suffix, suffix_lse = suffix_attention(queries, suffix_keys, suffix_values, lengths, scale)

    group = ctx * low
    everyone = merge(parts, suffix, suffix_lse, sessions, kv_local, group)
    everyone, weights, place = lax.optimization_barrier((everyone, weights, place))
    everyone = lax.all_to_all(everyone, ("ctx", "yl"), 0, 0, tiled=True)
    everyone = everyone.reshape(group * sessions, local_heads * dim)
    partial_out = project(place, everyone, weights, heads)
    partial_out = partial_out.reshape(heads * wide, group * sessions // heads, out_weight.shape[1])
    partial_out = lax.all_to_all(partial_out, ("yh", "core", "x"), 0, 0, tiled=True)
    partial_out = partial_out.reshape(heads, wide, group // heads, sessions, out_weight.shape[1])
    return finish(partial_out).reshape(group * sessions * wide // heads, out_weight.shape[1])


def solution(mesh):
    fine = Mesh(mesh.devices.reshape(8, 2, 2, 2, 4), ("ctx", "yh", "core", "yl", "x"))
    both = ("ctx",) + SESS
    return jax.shard_map(
        per_device,
        mesh=fine,
        in_specs=(
            P(both, HEAD, None),
            P(HEAD, "ctx", None),
            P(HEAD, "ctx", None),
            P(both, HEAD, None, None),
            P(both, HEAD, None, None),
            P(both),
            P(HEAD, both),
        ),
        out_specs=P(HEAD, both),
        check_vma=False,
    )
```

```python
import functools
import math

import jax
import jax.numpy as jnp
from jax import lax
from jax.experimental import pallas as pl
from jax.experimental.pallas import tpu as pltpu
from jax.sharding import Mesh
from jax.sharding import PartitionSpec as P

F32 = jnp.float32
BF16 = jnp.bfloat16
LOG2E = 1.4426950408889634
HEAD = ("yh", "core")
SESS = ("yl", "x")
NT = (((1,), (1,)), ((), ()))


def soft_tiles(scale, tiles, scores_of, values_of, acc_ref, finish):
    scores = scores_of(*tiles[0])
    for index, (span, part) in enumerate(tiles):
        following = tiles[index + 1] if index + 1 < len(tiles) else None
        ahead = scores_of(*following) if following else None
        new = jnp.max(scores, axis=1, keepdims=True)
        if part > 0:
            new = jnp.maximum(top, new)
            factor = jnp.exp2((top - new) * scale)
        weights = jnp.exp2((scores - new) * scale)
        share = jnp.sum(weights, axis=1, keepdims=True)
        product = jnp.dot(
            weights.astype(BF16), values_of(span, part), preferred_element_type=F32
        )
        if part > 0:
            total = total * factor + share
            product = acc_ref[span] * factor + product
        else:
            total = share
        top, scores = new, ahead
        if following is None or following[0] != span:
            finish(span, product / total, top * scale + jnp.log2(total))
        else:
            acc_ref[span] = product


def start_copies(block, sources, targets, sems):
    heads, length, _ = targets[0].shape
    for h in range(heads):
        for part in range(length // block):
            for source, target, sem in zip(sources, targets, sems):
                copy_part(block, source, target, sem, h, part).start()


def copy_part(block, source, target, sem, h, part):
    span = pl.ds(part * block, block)
    return pltpu.make_async_copy(source.at[h, span], target.at[h, span], sem.at[h, part])


def own_kernel(
    scale, block, q_ref, k_hbm, v_hbm, o_ref, lse_ref, k_ref, v_ref, acc_ref, k_sem, v_sem
):
    sessions, local_heads, dim = q_ref.shape
    heads, length, _ = k_ref.shape
    group = local_heads // heads
    rows = sessions * group
    parts = length // block

    start_copies(block, (k_hbm, v_hbm), (k_ref, v_ref), (k_sem, v_sem))

    def scores_of(span, part):
        h = span.start // rows
        copy_part(block, k_hbm, k_ref, k_sem, h, part).wait()
        q = q_ref[:, h * group : (h + 1) * group, :].reshape(rows, dim)
        keys = k_ref[h, part * block : (part + 1) * block]
        return lax.dot_general(q, keys, NT, preferred_element_type=F32)

    def values_of(span, part):
        h = span.start // rows
        copy_part(block, v_hbm, v_ref, v_sem, h, part).wait()
        return v_ref[h, part * block : (part + 1) * block]

    def finish(span, out, lse):
        h = span.start // rows
        o_ref[h] = out.astype(BF16)
        lse_ref[h] = jnp.broadcast_to(lse, (rows, dim))

    spans = [slice(h * rows, (h + 1) * rows) for h in range(heads)]
    tiles = [(span, part) for span in spans for part in range(parts)]
    soft_tiles(scale, tiles, scores_of, values_of, acc_ref, finish)


def own_attention(q, keys, values, scale):
    sessions, local_heads, dim = q.shape
    heads, length, _ = keys.shape
    rows = sessions * local_heads // heads
    block = length // 2
    vmem = pl.BlockSpec(memory_space=pltpu.VMEM)
    hbm = pl.BlockSpec(memory_space=pltpu.HBM)
    return pl.pallas_call(
        functools.partial(own_kernel, scale, block),
        in_specs=[vmem, hbm, hbm],
        out_specs=[vmem] * 2,
        out_shape=[
            jax.ShapeDtypeStruct((heads, rows, dim), BF16),
            jax.ShapeDtypeStruct((heads, rows, dim), F32),
        ],
        scratch_shapes=[
            pltpu.VMEM(keys.shape, BF16),
            pltpu.VMEM(values.shape, BF16),
            pltpu.VMEM((heads * rows, dim), F32),
            pltpu.SemaphoreType.DMA((heads, length // block)),
            pltpu.SemaphoreType.DMA((heads, length // block)),
        ],
        compiler_params=pltpu.CompilerParams(vmem_limit_bytes=24 << 20),
        cost_estimate=pl.CostEstimate(
            flops=4 * heads * rows * length * dim,
            bytes_accessed=4 * heads * length * dim,
            transcendentals=heads * rows * length,
        ),
        name="own_attention",
    )(
        q,
        pltpu.with_memory_space_constraint(keys, pltpu.HBM),
        pltpu.with_memory_space_constraint(values, pltpu.HBM),
    )


def prefix_kernel(
    scale, chunk, block, me_ref, all_q_ref, k_hbm, v_hbm, own_ref, own_lse_ref, o_ref,
    k_ref, v_ref, q_ref, acc_ref, lse_ref, k_sem, v_sem,
):
    head = pl.program_id(0)
    sources, sessions, local_heads, dim = all_q_ref.shape
    heads, length, _ = k_ref.shape
    group = local_heads // heads
    rows = sessions * group
    others = sources - 1
    place = [lax.rem(me_ref[0] + (1 + j), sources) for j in range(sources)]

    @pl.when(head == 0)
    def _():
        start_copies(block, (k_hbm, v_hbm), (k_ref, v_ref), (k_sem, v_sem))
        for j in range(others):
            for h in range(heads):
                part = all_q_ref[place[j], :, h * group : (h + 1) * group, :]
                q_ref[h, j * rows : (j + 1) * rows] = part.reshape(rows, dim)

    def scores_of(span, part):
        if span.start == 0:
            copy_part(block, k_hbm, k_ref, k_sem, head, part).wait()
        keys = k_ref[head, part * block : (part + 1) * block]
        return lax.dot_general(q_ref[head, span], keys, NT, preferred_element_type=F32)

    def values_of(span, part):
        if span.start == 0:
            copy_part(block, v_hbm, v_ref, v_sem, head, part).wait()
        return v_ref[head, part * block : (part + 1) * block]

    def finish(span, out, lse):
        lse_ref[head, span] = jnp.broadcast_to(lse, (lse.shape[0], lse_ref.shape[2]))
        out = out.astype(BF16)
        for i in range(out.shape[0] // rows):
            source = place[span.start // rows + i]
            o_ref[source, pl.ds(head * rows, rows), :] = out[i * rows : (i + 1) * rows]

    spans = [
        slice(j * rows, min(j + chunk, others) * rows) for j in range(0, others, chunk)
    ]
    tiles = [(span, part) for span in spans for part in range(length // block)]
    soft_tiles(scale, tiles, scores_of, values_of, acc_ref, finish)

    @pl.when(head == heads - 1)
    def _():
        for h in range(heads):
            o_ref[place[others], h * rows : (h + 1) * rows, :] = own_ref[h]
        for j in range(sources):
            pieces = [
                lse_ref[h, j * rows : (j + 1) * rows, :] if j < others else own_lse_ref[h]
                for h in range(heads)
            ]
            row = jnp.concatenate(pieces, axis=0).T[0:8]
            high = row.astype(BF16).astype(F32)
            middle = (row - high).astype(BF16).astype(F32)
            low = row - high - middle
            index = lax.broadcasted_iota(jnp.int32, row.shape, 0)
            stats = jnp.where(index == 0, high, jnp.where(index == 1, middle, low))
            o_ref[place[j], heads * rows : heads * rows + 8, :] = stats.astype(BF16)


def prefix_attention(me, q, keys, values, own, own_lse, scale):
    sources, sessions, local_heads, dim = q.shape
    heads, length, _ = keys.shape
    rows = sessions * local_heads // heads
    block = length // 2
    other_rows = (sources - 1) * rows

    def whole(shape):
        return pl.BlockSpec(shape, lambda h: (0,) * len(shape))

    return pl.pallas_call(
        functools.partial(prefix_kernel, scale, 2, block),
        grid=(heads,),
        in_specs=[
            pl.BlockSpec(memory_space=pltpu.SMEM),
            whole(q.shape),
            pl.BlockSpec(memory_space=pltpu.HBM),
            pl.BlockSpec(memory_space=pltpu.HBM),
            whole(own.shape),
            whole(own_lse.shape),
        ],
        out_specs=whole((sources, heads * rows + 8, dim)),
        out_shape=jax.ShapeDtypeStruct((sources, heads * rows + 8, dim), BF16),
        scratch_shapes=[
            pltpu.VMEM(keys.shape, BF16),
            pltpu.VMEM(values.shape, BF16),
            pltpu.VMEM((heads, other_rows, dim), BF16),
            pltpu.VMEM((other_rows, dim), F32),
            pltpu.VMEM((heads, other_rows, 128), F32),
            pltpu.SemaphoreType.DMA((heads, length // block)),
            pltpu.SemaphoreType.DMA((heads, length // block)),
        ],
        compiler_params=pltpu.CompilerParams(
            dimension_semantics=("arbitrary",), vmem_limit_bytes=32 << 20
        ),
        cost_estimate=pl.CostEstimate(
            flops=4 * heads * other_rows * length * dim,
            bytes_accessed=4 * heads * length * dim,
            transcendentals=heads * other_rows * length,
        ),
        name="prefix_attention",
    )(
        me,
        q,
        pltpu.with_memory_space_constraint(keys, pltpu.HBM),
        pltpu.with_memory_space_constraint(values, pltpu.HBM),
        own,
        own_lse,
    )


def suffix_kernel(scale, lengths_ref, q_ref, k_ref, v_ref, o_ref, lse_ref):
    step = pl.program_id(0)
    count, heads, length = k_ref.shape[0], k_ref.shape[1], k_ref.shape[2]
    group = q_ref.shape[1] // heads
    sessions = pl.num_programs(0) * count
    pairs = [(s, h) for s in range(count) for h in range(heads)]
    all_scores = [
        lax.dot_general(
            q_ref[s, h * group : (h + 1) * group], k_ref[s, h], NT, preferred_element_type=F32
        )
        for s, h in pairs
    ]
    position = lax.broadcasted_iota(jnp.int32, (group, length), 1)
    softened = []
    for (s, h), scores in zip(pairs, all_scores):
        scores = jnp.where(position < lengths_ref[step * count + s], scores, -1e30)
        top = jnp.max(scores, axis=1, keepdims=True)
        weights = jnp.exp2((scores - top) * scale)
        softened.append((top, jnp.sum(weights, axis=1, keepdims=True), weights.astype(BF16)))
    for (s, h), (top, total, weights) in zip(pairs, softened):
        out = jnp.dot(weights, v_ref[s, h], preferred_element_type=F32) / total
        rows = pl.ds((h * sessions + step * count + s) * group, group)
        o_ref[rows, :] = out
        lse_ref[rows, :] = jnp.broadcast_to(top * scale + jnp.log2(total), out.shape)


def suffix_attention(q, keys, values, lengths, scale):
    sessions, heads, length, dim = keys.shape
    rows = q.shape[1] * sessions
    count = 4
    spec = pl.BlockSpec((rows, dim), lambda s, n: (0, 0))
    return pl.pallas_call(
        functools.partial(suffix_kernel, scale),
        grid_spec=pltpu.PrefetchScalarGridSpec(
            num_scalar_prefetch=1,
            grid=(sessions // count,),
            in_specs=[
                pl.BlockSpec((count,) + q.shape[1:], lambda s, n: (s, 0, 0)),
                pl.BlockSpec((count, heads, length, dim), lambda s, n: (s, 0, 0, 0)),
                pl.BlockSpec((count, heads, length, dim), lambda s, n: (s, 0, 0, 0)),
            ],
            out_specs=[spec, spec],
        ),
        out_shape=[jax.ShapeDtypeStruct((rows, dim), F32)] * 2,
        compiler_params=pltpu.CompilerParams(vmem_limit_bytes=16 << 20),
        cost_estimate=pl.CostEstimate(
            flops=4 * rows * length * dim,
            bytes_accessed=4 * sessions * heads * length * dim,
            transcendentals=rows * length,
        ),
        name="suffix_attention",
    )(
        lengths,
        q,
        pltpu.with_memory_space_constraint(keys, pltpu.HBM),
        pltpu.with_memory_space_constraint(values, pltpu.HBM),
    )


def merge_kernel(heads, parts_ref, suffix_ref, suffix_lse_ref, out_ref, result_ref):
    sources, padded, dim = parts_ref.shape
    rows = padded - 8
    copies, sessions, _ = out_ref.shape
    stats = []
    for c in range(sources):
        three = parts_ref[c, rows : rows + 8, :].astype(F32)
        stats.append(three[0:1] + three[1:2] + three[2:3])
    filler = jnp.full((rows - sources, rows), -3e38, F32)
    table = jnp.concatenate(stats + [filler], axis=0).T
    own = suffix_lse_ref[...]
    top = jnp.maximum(jnp.max(table, axis=1, keepdims=True), own[:, 0:1])
    shares = jnp.exp2(table - top)
    own_share = jnp.exp2(own[:, 0:1] - top)
    total = jnp.sum(shares, axis=1, keepdims=True) + own_share
    result = own_share * suffix_ref[...]
    for c in range(sources):
        result += shares[:, c : c + 1] * parts_ref[c, 0:rows, :].astype(F32)
    result_ref[...] = result / total
    group = rows // sessions // heads
    for h in range(heads):
        for g in range(group):
            first = h * sessions * group + g
            piece = result_ref[pl.ds(first, sessions, stride=group), :].astype(BF16)
            column = (h * group + g) * dim
            for copy in range(copies):
                out_ref[copy, :, column : column + dim] = piece


def merge(parts, suffix, suffix_lse, sessions, heads, copies):
    rows, dim = suffix.shape
    return pl.pallas_call(
        functools.partial(merge_kernel, heads),
        scratch_shapes=[pltpu.VMEM((rows, dim), F32)],
        compiler_params=pltpu.CompilerParams(vmem_limit_bytes=16 << 20),
        out_shape=jax.ShapeDtypeStruct((copies, sessions, rows // sessions * dim), BF16),
        name="merge_shards",
    )(parts, suffix, suffix_lse)


def project_kernel(place_ref, attended_ref, *refs):
    weights, out_ref = refs[:-1], refs[-1]
    heads, wide, rows, columns = out_ref.shape
    for k, weight_ref in enumerate(weights):
        product = jnp.dot(attended_ref[...], weight_ref[...], preferred_element_type=F32)
        x = lax.rem(place_ref[0] + (wide - k), wide)
        out_ref[:, x] = product.astype(BF16).reshape(heads, rows, columns)


def project(place, attended, weights, heads):
    sessions, features = attended.shape
    columns = weights[0].shape[1]
    vmem = pl.BlockSpec(memory_space=pltpu.VMEM)
    return pl.pallas_call(
        project_kernel,
        in_specs=[pl.BlockSpec(memory_space=pltpu.SMEM)] + [vmem] * (1 + len(weights)),
        out_specs=vmem,
        out_shape=jax.ShapeDtypeStruct((heads, len(weights), sessions // heads, columns), BF16),
        compiler_params=pltpu.CompilerParams(vmem_limit_bytes=16 << 20),
        name="project",
    )(place, attended, *weights)


def finish_kernel(parts_ref, out_ref):
    for x in range(parts_ref.shape[1]):
        total = parts_ref[0, x].astype(F32)
        for h in range(1, parts_ref.shape[0]):
            total += parts_ref[h, x].astype(F32)
        out_ref[:, x] = total


def finish(parts):
    _, x, outer, sessions, columns = parts.shape
    return pl.pallas_call(
        finish_kernel,
        out_shape=jax.ShapeDtypeStruct((outer, x, sessions, columns), F32),
        compiler_params=pltpu.CompilerParams(vmem_limit_bytes=16 << 20),
        name="sum_heads",
    )(parts)


def per_device(queries, prefix_keys, prefix_values, suffix_keys, suffix_values, lengths, out_weight):
    sessions, local_heads, dim = queries.shape
    kv_local = prefix_keys.shape[0]
    scale = LOG2E / math.sqrt(dim)
    ctx = lax.axis_size("ctx")
    heads = lax.axis_size("yh") * lax.axis_size("core")
    wide = lax.axis_size("x")
    low = lax.axis_size("yl")

    flat = queries.reshape(1, sessions * local_heads, dim)
    spread = jnp.broadcast_to(flat, (ctx, sessions * local_heads, dim))
    gathered = lax.all_to_all(spread, "ctx", 0, 0, tiled=True)
    gathered = gathered.reshape(ctx, sessions, local_heads, dim)
    weights = [out_weight]
    for k in range(1, wide):
        pairs = [(x, (x + k) % wide) for x in range(wide)]
        weights.append(lax.ppermute(out_weight, "x", pairs))

    own, own_lse = own_attention(queries, prefix_keys, prefix_values, scale)
    me = lax.axis_index("ctx").astype(jnp.int32).reshape(1)
    parts = prefix_attention(
        me, gathered, prefix_keys, prefix_values, own, own_lse, scale
    )
    place = lax.axis_index("x").astype(jnp.int32).reshape(1)
    parts, queries, place = lax.optimization_barrier((parts, queries, place))
    parts = lax.all_to_all(parts, "ctx", 0, 0, tiled=True)
    suffix, suffix_lse = suffix_attention(queries, suffix_keys, suffix_values, lengths, scale)

    group = ctx * low
    everyone = merge(parts, suffix, suffix_lse, sessions, kv_local, group)
    everyone, weights, place = lax.optimization_barrier((everyone, weights, place))
    everyone = lax.all_to_all(everyone, ("ctx", "yl"), 0, 0, tiled=True)
    everyone = everyone.reshape(group * sessions, local_heads * dim)
    partial_out = project(place, everyone, weights, heads)
    partial_out = partial_out.reshape(heads * wide, group * sessions // heads, out_weight.shape[1])
    partial_out = lax.all_to_all(partial_out, ("yh", "core", "x"), 0, 0, tiled=True)
    partial_out = partial_out.reshape(heads, wide, group // heads, sessions, out_weight.shape[1])
    return finish(partial_out).reshape(group * sessions * wide // heads, out_weight.shape[1])


def solution(mesh):
    fine = Mesh(mesh.devices.reshape(8, 2, 2, 2, 4), ("ctx", "yh", "core", "yl", "x"))
    both = ("ctx",) + SESS
    return jax.shard_map(
        per_device,
        mesh=fine,
        in_specs=(
            P(both, HEAD, None),
            P(HEAD, "ctx", None),
            P(HEAD, "ctx", None),
            P(both, HEAD, None, None),
            P(both, HEAD, None, None),
            P(both),
            P(HEAD, both),
        ),
        out_specs=P(HEAD, both),
        check_vma=False,
    )
```

```python
import functools
import math

import jax
import jax.numpy as jnp
from jax import lax
from jax.experimental import pallas as pl
from jax.experimental.pallas import tpu as pltpu
from jax.sharding import Mesh
from jax.sharding import PartitionSpec as P

F32 = jnp.float32
BF16 = jnp.bfloat16
LOG2E = 1.4426950408889634
HEAD = ("yh", "core")
SESS = ("yl", "x")
NT = (((1,), (1,)), ((), ()))


TN = (((0,), (0,)), ((), ()))
SAFE_TOTAL = 2.0**100


def prefix_kernel(
    scale, tile, first, all_q_ref, k_hbm, v_hbm, o_ref, q_ref, k_ref, v_ref, acc_ref, top_ref,
    total_ref, lse_ref, k_sem, v_sem,
):
    head = pl.program_id(0)
    sources, sessions, local_heads, dim = all_q_ref.shape
    heads, length, _ = k_ref.shape
    group = local_heads // heads
    rows = sessions * group
    parts = [(0, first), (first, length - first)]

    def copy_of(source, target, sem, h, part):
        span = pl.ds(*parts[part])
        return pltpu.make_async_copy(source.at[h, span], target.at[h, span], sem.at[h, part])

    @pl.when(head == 0)
    def _():
        for h in range(heads):
            for part in range(len(parts)):
                copy_of(k_hbm, k_ref, k_sem, h, part).start()
                copy_of(v_hbm, v_ref, v_sem, h, part).start()
        for h in range(heads):
            part = all_q_ref[:, :, h * group : (h + 1) * group, :]
            q_ref[h] = part.reshape(sources * rows, dim)

    def scores_of(start):
        keys = k_ref[head, pl.ds(start, tile), :]
        return lax.dot_general(keys, q_ref[head], NT, preferred_element_type=F32)

    def product_of(weights, start):
        values = v_ref[head, pl.ds(start, tile), :]
        return lax.dot_general(values, weights.astype(BF16), TN, preferred_element_type=F32)

    copy_of(k_hbm, k_ref, k_sem, head, 0).wait()
    scores = scores_of(0)
    top = jnp.max(scores, axis=0, keepdims=True)
    for start in range(0, length, tile):
        if start == 0:
            copy_of(v_hbm, v_ref, v_sem, head, 0).wait()
        if start == first:
            copy_of(v_hbm, v_ref, v_sem, head, 1).wait()
        if start + tile == first:
            copy_of(k_hbm, k_ref, k_sem, head, 1).wait()
        ahead = scores_of(start + tile) if start + tile < length else None
        weights = jnp.exp2((scores - top) * scale)
        share = jnp.sum(weights, axis=0, keepdims=True)
        product = product_of(weights, start)
        if start == 0:
            total = share
            acc_ref[...] = product
        else:
            total = total + share
            acc_ref[...] = acc_ref[...] + product
        scores = ahead
    top_ref[...] = top
    total_ref[...] = total

    unsafe = jnp.max(jnp.where(total <= SAFE_TOTAL, 0.0, 1.0))

    @pl.when(unsafe > 0.0)
    def _():
        top_ref[...] = jnp.full_like(top_ref, -1e30)
        total_ref[...] = jnp.zeros_like(total_ref)
        acc_ref[...] = jnp.zeros_like(acc_ref)

        def step(index, carry):
            start = pl.multiple_of(index * tile, tile)
            scores = scores_of(start)
            old = top_ref[...]
            new = jnp.maximum(old, jnp.max(scores, axis=0, keepdims=True))
            factor = jnp.exp2((old - new) * scale)
            weights = jnp.exp2((scores - new) * scale)
            total_ref[...] = total_ref[...] * factor + jnp.sum(weights, axis=0, keepdims=True)
            acc_ref[...] = acc_ref[...] * factor + product_of(weights, start)
            top_ref[...] = new
            return carry

        lax.fori_loop(0, length // tile, step, 0)

    out = (acc_ref[...] / total_ref[...]).T.astype(BF16)
    lse_ref[head] = jnp.broadcast_to(
        top_ref[...] * scale + jnp.log2(total_ref[...]), lse_ref.shape[1:]
    )
    for c in range(sources):
        o_ref[c, pl.ds(head * rows, rows), :] = out[c * rows : (c + 1) * rows]

    @pl.when(head == heads - 1)
    def _():
        for c in range(sources):
            row = jnp.concatenate(
                [lse_ref[h, :, c * rows : (c + 1) * rows] for h in range(heads)], axis=1
            )
            high = row.astype(BF16).astype(F32)
            middle = (row - high).astype(BF16).astype(F32)
            low = row - high - middle
            place = lax.broadcasted_iota(jnp.int32, row.shape, 0)
            stats = jnp.where(place == 0, high, jnp.where(place == 1, middle, low))
            o_ref[c, heads * rows : heads * rows + 8, :] = stats.astype(BF16)


def prefix_attention(q, keys, values, scale):
    sources, sessions, local_heads, dim = q.shape
    heads, length, _ = keys.shape
    rows = sessions * local_heads // heads
    total_rows = sources * rows
    return pl.pallas_call(
        functools.partial(prefix_kernel, scale, length // 12, length // 6),
        grid=(heads,),
        in_specs=[
            pl.BlockSpec(q.shape, lambda h: (0, 0, 0, 0)),
            pl.BlockSpec(memory_space=pltpu.HBM),
            pl.BlockSpec(memory_space=pltpu.HBM),
        ],
        out_specs=pl.BlockSpec((sources, heads * rows + 8, dim), lambda h: (0, 0, 0)),
        out_shape=jax.ShapeDtypeStruct((sources, heads * rows + 8, dim), BF16),
        scratch_shapes=[
            pltpu.VMEM((heads, total_rows, dim), BF16),
            pltpu.VMEM(keys.shape, BF16),
            pltpu.VMEM(values.shape, BF16),
            pltpu.VMEM((dim, total_rows), F32),
            pltpu.VMEM((1, total_rows), F32),
            pltpu.VMEM((1, total_rows), F32),
            pltpu.VMEM((heads, 8, total_rows), F32),
            pltpu.SemaphoreType.DMA((heads, 2)),
            pltpu.SemaphoreType.DMA((heads, 2)),
        ],
        compiler_params=pltpu.CompilerParams(
            dimension_semantics=("arbitrary",), vmem_limit_bytes=32 << 20
        ),
        cost_estimate=pl.CostEstimate(
            flops=4 * heads * total_rows * length * dim,
            bytes_accessed=4 * heads * length * dim,
            transcendentals=heads * total_rows * length,
        ),
        name="prefix_attention",
    )(
        q,
        pltpu.with_memory_space_constraint(keys, pltpu.HBM),
        pltpu.with_memory_space_constraint(values, pltpu.HBM),
    )


def suffix_kernel(scale, lengths_ref, q_ref, k_ref, v_ref, o_ref, lse_ref):
    step = pl.program_id(0)
    count, heads, length = k_ref.shape[0], k_ref.shape[1], k_ref.shape[2]
    group = q_ref.shape[1] // heads
    sessions = pl.num_programs(0) * count
    pairs = [(s, h) for s in range(count) for h in range(heads)]
    all_scores = [
        lax.dot_general(
            q_ref[s, h * group : (h + 1) * group], k_ref[s, h], NT, preferred_element_type=F32
        )
        for s, h in pairs
    ]
    position = lax.broadcasted_iota(jnp.int32, (group, length), 1)
    softened = []
    for (s, h), scores in zip(pairs, all_scores):
        scores = jnp.where(position < lengths_ref[step * count + s], scores, -1e30)
        top = jnp.max(scores, axis=1, keepdims=True)
        weights = jnp.exp2((scores - top) * scale)
        softened.append((top, jnp.sum(weights, axis=1, keepdims=True), weights.astype(BF16)))
    for (s, h), (top, total, weights) in zip(pairs, softened):
        out = jnp.dot(weights, v_ref[s, h], preferred_element_type=F32) / total
        rows = pl.ds((h * sessions + step * count + s) * group, group)
        o_ref[rows, :] = out
        lse_ref[rows, :] = jnp.broadcast_to(top * scale + jnp.log2(total), out.shape)


def suffix_attention(q, keys, values, lengths, scale):
    sessions, heads, length, dim = keys.shape
    rows = q.shape[1] * sessions
    count = 4
    spec = pl.BlockSpec((rows, dim), lambda s, n: (0, 0))
    return pl.pallas_call(
        functools.partial(suffix_kernel, scale),
        grid_spec=pltpu.PrefetchScalarGridSpec(
            num_scalar_prefetch=1,
            grid=(sessions // count,),
            in_specs=[
                pl.BlockSpec((count,) + q.shape[1:], lambda s, n: (s, 0, 0)),
                pl.BlockSpec((count, heads, length, dim), lambda s, n: (s, 0, 0, 0)),
                pl.BlockSpec((count, heads, length, dim), lambda s, n: (s, 0, 0, 0)),
            ],
            out_specs=[spec, spec],
        ),
        out_shape=[jax.ShapeDtypeStruct((rows, dim), F32)] * 2,
        compiler_params=pltpu.CompilerParams(vmem_limit_bytes=16 << 20),
        cost_estimate=pl.CostEstimate(
            flops=4 * rows * length * dim,
            bytes_accessed=4 * sessions * heads * length * dim,
            transcendentals=rows * length,
        ),
        name="suffix_attention",
    )(
        lengths,
        q,
        pltpu.with_memory_space_constraint(keys, pltpu.HBM),
        pltpu.with_memory_space_constraint(values, pltpu.HBM),
    )


def merge_kernel(heads, parts_ref, suffix_ref, suffix_lse_ref, out_ref, result_ref):
    sources, padded, dim = parts_ref.shape
    rows = padded - 8
    copies, sessions, _ = out_ref.shape
    stats = []
    for c in range(sources):
        three = parts_ref[c, rows : rows + 8, :].astype(F32)
        stats.append(three[0:1] + three[1:2] + three[2:3])
    filler = jnp.full((rows - sources, rows), -3e38, F32)
    table = jnp.concatenate(stats + [filler], axis=0).T
    own = suffix_lse_ref[...]
    top = jnp.maximum(jnp.max(table, axis=1, keepdims=True), own[:, 0:1])
    shares = jnp.exp2(table - top)
    own_share = jnp.exp2(own[:, 0:1] - top)
    total = jnp.sum(shares, axis=1, keepdims=True) + own_share
    result = own_share * suffix_ref[...]
    for c in range(sources):
        result += shares[:, c : c + 1] * parts_ref[c, 0:rows, :].astype(F32)
    result_ref[...] = result / total
    group = rows // sessions // heads
    for h in range(heads):
        for g in range(group):
            first = h * sessions * group + g
            piece = result_ref[pl.ds(first, sessions, stride=group), :].astype(BF16)
            column = (h * group + g) * dim
            for copy in range(copies):
                out_ref[copy, :, column : column + dim] = piece


def merge(parts, suffix, suffix_lse, sessions, heads, copies):
    rows, dim = suffix.shape
    return pl.pallas_call(
        functools.partial(merge_kernel, heads),
        scratch_shapes=[pltpu.VMEM((rows, dim), F32)],
        compiler_params=pltpu.CompilerParams(vmem_limit_bytes=16 << 20),
        out_shape=jax.ShapeDtypeStruct((copies, sessions, rows // sessions * dim), BF16),
        name="merge_shards",
    )(parts, suffix, suffix_lse)


def project_kernel(place_ref, attended_ref, *refs):
    weights, out_ref = refs[:-1], refs[-1]
    heads, wide, rows, columns = out_ref.shape
    for k, weight_ref in enumerate(weights):
        product = jnp.dot(attended_ref[...], weight_ref[...], preferred_element_type=F32)
        x = lax.rem(place_ref[0] + (wide - k), wide)
        out_ref[:, x] = product.astype(BF16).reshape(heads, rows, columns)


def project(place, attended, weights, heads):
    sessions, features = attended.shape
    columns = weights[0].shape[1]
    vmem = pl.BlockSpec(memory_space=pltpu.VMEM)
    return pl.pallas_call(
        project_kernel,
        in_specs=[pl.BlockSpec(memory_space=pltpu.SMEM)] + [vmem] * (1 + len(weights)),
        out_specs=vmem,
        out_shape=jax.ShapeDtypeStruct((heads, len(weights), sessions // heads, columns), BF16),
        compiler_params=pltpu.CompilerParams(vmem_limit_bytes=16 << 20),
        name="project",
    )(place, attended, *weights)


def finish_kernel(parts_ref, out_ref):
    for x in range(parts_ref.shape[1]):
        total = parts_ref[0, x].astype(F32)
        for h in range(1, parts_ref.shape[0]):
            total += parts_ref[h, x].astype(F32)
        out_ref[:, x] = total


def finish(parts):
    _, x, outer, sessions, columns = parts.shape
    return pl.pallas_call(
        finish_kernel,
        out_shape=jax.ShapeDtypeStruct((outer, x, sessions, columns), F32),
        compiler_params=pltpu.CompilerParams(vmem_limit_bytes=16 << 20),
        name="sum_heads",
    )(parts)


def spread_kernel(q_ref, out_ref, sem):
    copies = [
        pltpu.make_async_copy(q_ref, out_ref.at[c], sem.at[c]) for c in range(out_ref.shape[0])
    ]
    for copy in copies:
        copy.start()
    for copy in copies:
        copy.wait()


def spread(queries, copies):
    return pl.pallas_call(
        spread_kernel,
        in_specs=[pl.BlockSpec(memory_space=pl.ANY)],
        out_specs=pl.BlockSpec(memory_space=pl.ANY),
        out_shape=jax.ShapeDtypeStruct((copies,) + queries.shape, queries.dtype),
        scratch_shapes=[pltpu.SemaphoreType.DMA((copies,))],
        name="spread_queries",
    )(queries)


def per_device(queries, prefix_keys, prefix_values, suffix_keys, suffix_values, lengths, out_weight):
    sessions, local_heads, dim = queries.shape
    kv_local = prefix_keys.shape[0]
    scale = LOG2E / math.sqrt(dim)
    ctx = lax.axis_size("ctx")
    heads = lax.axis_size("yh") * lax.axis_size("core")
    wide = lax.axis_size("x")
    low = lax.axis_size("yl")

    gathered = lax.all_to_all(spread(queries, ctx), "ctx", 0, 0, tiled=False)
    weights = [out_weight]
    for k in range(1, wide):
        pairs = [(x, (x + k) % wide) for x in range(wide)]
        weights.append(lax.ppermute(out_weight, "x", pairs))

    parts = prefix_attention(gathered, prefix_keys, prefix_values, scale)
    place = lax.axis_index("x").astype(jnp.int32).reshape(1)
    parts, queries, place = lax.optimization_barrier((parts, queries, place))
    parts = lax.all_to_all(parts, "ctx", 0, 0, tiled=True)
    suffix, suffix_lse = suffix_attention(queries, suffix_keys, suffix_values, lengths, scale)

    group = ctx * low
    everyone = merge(parts, suffix, suffix_lse, sessions, kv_local, group)
    everyone, weights, place = lax.optimization_barrier((everyone, weights, place))
    everyone = lax.all_to_all(everyone, ("ctx", "yl"), 0, 0, tiled=True)
    everyone = everyone.reshape(group * sessions, local_heads * dim)
    partial_out = project(place, everyone, weights, heads)
    partial_out = partial_out.reshape(heads * wide, group * sessions // heads, out_weight.shape[1])
    partial_out = lax.all_to_all(partial_out, ("yh", "core", "x"), 0, 0, tiled=True)
    partial_out = partial_out.reshape(heads, wide, group // heads, sessions, out_weight.shape[1])
    return finish(partial_out).reshape(group * sessions * wide // heads, out_weight.shape[1])


def solution(mesh):
    fine = Mesh(mesh.devices.reshape(8, 2, 2, 2, 4), ("ctx", "yh", "core", "yl", "x"))
    both = ("ctx",) + SESS
    return jax.shard_map(
        per_device,
        mesh=fine,
        in_specs=(
            P(both, HEAD, None),
            P(HEAD, "ctx", None),
            P(HEAD, "ctx", None),
            P(both, HEAD, None, None),
            P(both, HEAD, None, None),
            P(both),
            P(HEAD, both),
        ),
        out_specs=P(HEAD, both),
        check_vma=False,
    )
```

```python
import functools
import math

import jax
import jax.numpy as jnp
from jax import lax
from jax.experimental import pallas as pl
from jax.experimental.pallas import tpu as pltpu
from jax.sharding import Mesh
from jax.sharding import PartitionSpec as P

F32 = jnp.float32
BF16 = jnp.bfloat16
LOG2E = 1.4426950408889634
HEAD = ("yh", "core")
SESS = ("yl", "x")
NT = (((1,), (1,)), ((), ()))


TN = (((0,), (0,)), ((), ()))
SAFE_TOTAL = 2.0**100


def prefix_kernel(
    scale, tile, first, all_q_ref, k_hbm, v_hbm, o_ref, q_ref, k_ref, v_ref, acc_ref, top_ref,
    total_ref, lse_ref, k_sem, v_sem,
):
    head = pl.program_id(0)
    sources, sessions, local_heads, dim = all_q_ref.shape
    heads, length, _ = k_ref.shape
    group = local_heads // heads
    rows = sessions * group
    parts = [(0, first), (first, length - first)]

    def copy_of(source, target, sem, h, part):
        span = pl.ds(*parts[part])
        return pltpu.make_async_copy(source.at[h, span], target.at[h, span], sem.at[h, part])

    @pl.when(head == 0)
    def _():
        for h in range(heads):
            for part in range(len(parts)):
                copy_of(k_hbm, k_ref, k_sem, h, part).start()
                copy_of(v_hbm, v_ref, v_sem, h, part).start()
        for h in range(heads):
            part = all_q_ref[:, :, h * group : (h + 1) * group, :]
            q_ref[h] = part.reshape(sources * rows, dim)

    def scores_of(start):
        keys = k_ref[head, pl.ds(start, tile), :]
        return lax.dot_general(keys, q_ref[head], NT, preferred_element_type=F32)

    def product_of(weights, start):
        values = v_ref[head, pl.ds(start, tile), :]
        return lax.dot_general(values, weights.astype(BF16), TN, preferred_element_type=F32)

    copy_of(k_hbm, k_ref, k_sem, head, 0).wait()
    scores = scores_of(0)
    top = jnp.max(scores, axis=0, keepdims=True)
    for start in range(0, length, tile):
        if start == 0:
            copy_of(v_hbm, v_ref, v_sem, head, 0).wait()
        if start == first:
            copy_of(v_hbm, v_ref, v_sem, head, 1).wait()
        if start + tile == first:
            copy_of(k_hbm, k_ref, k_sem, head, 1).wait()
        ahead = scores_of(start + tile) if start + tile < length else None
        weights = jnp.exp2((scores - top) * scale)
        share = jnp.sum(weights, axis=0, keepdims=True)
        product = product_of(weights, start)
        if start == 0:
            total = share
            acc_ref[...] = product
        else:
            total = total + share
            acc_ref[...] = acc_ref[...] + product
        scores = ahead
    top_ref[...] = top
    total_ref[...] = total

    unsafe = jnp.max(jnp.where(total <= SAFE_TOTAL, 0.0, 1.0))

    @pl.when(unsafe > 0.0)
    def _():
        top_ref[...] = jnp.full_like(top_ref, -1e30)
        total_ref[...] = jnp.zeros_like(total_ref)
        acc_ref[...] = jnp.zeros_like(acc_ref)

        def step(index, carry):
            start = pl.multiple_of(index * tile, tile)
            scores = scores_of(start)
            old = top_ref[...]
            new = jnp.maximum(old, jnp.max(scores, axis=0, keepdims=True))
            factor = jnp.exp2((old - new) * scale)
            weights = jnp.exp2((scores - new) * scale)
            total_ref[...] = total_ref[...] * factor + jnp.sum(weights, axis=0, keepdims=True)
            acc_ref[...] = acc_ref[...] * factor + product_of(weights, start)
            top_ref[...] = new
            return carry

        lax.fori_loop(0, length // tile, step, 0)

    out = (acc_ref[...] / total_ref[...]).T.astype(BF16)
    lse_ref[head] = jnp.broadcast_to(
        top_ref[...] * scale + jnp.log2(total_ref[...]), lse_ref.shape[1:]
    )
    for c in range(sources):
        o_ref[c, pl.ds(head * rows, rows), :] = out[c * rows : (c + 1) * rows]

    @pl.when(head == heads - 1)
    def _():
        for c in range(sources):
            row = jnp.concatenate(
                [lse_ref[h, :, c * rows : (c + 1) * rows] for h in range(heads)], axis=1
            )
            high = row.astype(BF16).astype(F32)
            middle = (row - high).astype(BF16).astype(F32)
            low = row - high - middle
            place = lax.broadcasted_iota(jnp.int32, row.shape, 0)
            stats = jnp.where(place == 0, high, jnp.where(place == 1, middle, low))
            o_ref[c, heads * rows : heads * rows + 8, :] = stats.astype(BF16)


def prefix_attention(q, keys, values, scale):
    sources, sessions, local_heads, dim = q.shape
    heads, length, _ = keys.shape
    rows = sessions * local_heads // heads
    total_rows = sources * rows
    return pl.pallas_call(
        functools.partial(prefix_kernel, scale, length // 12, length // 6),
        grid=(heads,),
        in_specs=[
            pl.BlockSpec(q.shape, lambda h: (0, 0, 0, 0)),
            pl.BlockSpec(memory_space=pltpu.HBM),
            pl.BlockSpec(memory_space=pltpu.HBM),
        ],
        out_specs=pl.BlockSpec((sources, heads * rows + 8, dim), lambda h: (0, 0, 0)),
        out_shape=jax.ShapeDtypeStruct((sources, heads * rows + 8, dim), BF16),
        scratch_shapes=[
            pltpu.VMEM((heads, total_rows, dim), BF16),
            pltpu.VMEM(keys.shape, BF16),
            pltpu.VMEM(values.shape, BF16),
            pltpu.VMEM((dim, total_rows), F32),
            pltpu.VMEM((1, total_rows), F32),
            pltpu.VMEM((1, total_rows), F32),
            pltpu.VMEM((heads, 8, total_rows), F32),
            pltpu.SemaphoreType.DMA((heads, 2)),
            pltpu.SemaphoreType.DMA((heads, 2)),
        ],
        compiler_params=pltpu.CompilerParams(
            dimension_semantics=("arbitrary",), vmem_limit_bytes=32 << 20
        ),
        cost_estimate=pl.CostEstimate(
            flops=4 * heads * total_rows * length * dim,
            bytes_accessed=4 * heads * length * dim,
            transcendentals=heads * total_rows * length,
        ),
        name="prefix_attention",
    )(
        q,
        pltpu.with_memory_space_constraint(keys, pltpu.HBM),
        pltpu.with_memory_space_constraint(values, pltpu.HBM),
    )


def suffix_kernel(scale, lengths_ref, q_ref, k_ref, v_ref, o_ref, lse_ref):
    step = pl.program_id(0)
    count, heads, length = k_ref.shape[0], k_ref.shape[1], k_ref.shape[2]
    group = q_ref.shape[1] // heads
    sessions = pl.num_programs(0) * count
    pairs = [(s, h) for s in range(count) for h in range(heads)]
    all_scores = [
        lax.dot_general(
            q_ref[s, h * group : (h + 1) * group], k_ref[s, h], NT, preferred_element_type=F32
        )
        for s, h in pairs
    ]
    position = lax.broadcasted_iota(jnp.int32, (group, length), 1)
    softened = []
    for (s, h), scores in zip(pairs, all_scores):
        scores = jnp.where(position < lengths_ref[step * count + s], scores, -1e30)
        top = jnp.max(scores, axis=1, keepdims=True)
        weights = jnp.exp2((scores - top) * scale)
        softened.append((top, jnp.sum(weights, axis=1, keepdims=True), weights.astype(BF16)))
    for (s, h), (top, total, weights) in zip(pairs, softened):
        out = jnp.dot(weights, v_ref[s, h], preferred_element_type=F32) / total
        rows = pl.ds((h * sessions + step * count + s) * group, group)
        o_ref[rows, :] = out
        lse_ref[rows, :] = jnp.broadcast_to(top * scale + jnp.log2(total), out.shape)


def suffix_attention(q, keys, values, lengths, scale):
    sessions, heads, length, dim = keys.shape
    rows = q.shape[1] * sessions
    count = 4
    spec = pl.BlockSpec((rows, dim), lambda s, n: (0, 0))
    return pl.pallas_call(
        functools.partial(suffix_kernel, scale),
        grid_spec=pltpu.PrefetchScalarGridSpec(
            num_scalar_prefetch=1,
            grid=(sessions // count,),
            in_specs=[
                pl.BlockSpec((count,) + q.shape[1:], lambda s, n: (s, 0, 0)),
                pl.BlockSpec((count, heads, length, dim), lambda s, n: (s, 0, 0, 0)),
                pl.BlockSpec((count, heads, length, dim), lambda s, n: (s, 0, 0, 0)),
            ],
            out_specs=[spec, spec],
        ),
        out_shape=[jax.ShapeDtypeStruct((rows, dim), F32)] * 2,
        compiler_params=pltpu.CompilerParams(vmem_limit_bytes=16 << 20),
        cost_estimate=pl.CostEstimate(
            flops=4 * rows * length * dim,
            bytes_accessed=4 * sessions * heads * length * dim,
            transcendentals=rows * length,
        ),
        name="suffix_attention",
    )(
        lengths,
        q,
        pltpu.with_memory_space_constraint(keys, pltpu.HBM),
        pltpu.with_memory_space_constraint(values, pltpu.HBM),
    )


def merge_kernel(heads, parts_ref, suffix_ref, suffix_lse_ref, out_ref, result_ref):
    sources, padded, dim = parts_ref.shape
    rows = padded - 8
    copies, sessions, _ = out_ref.shape
    stats = []
    for c in range(sources):
        three = parts_ref[c, rows : rows + 8, :].astype(F32)
        stats.append(three[0:1] + three[1:2] + three[2:3])
    filler = jnp.full((rows - sources, rows), -3e38, F32)
    table = jnp.concatenate(stats + [filler], axis=0).T
    own = suffix_lse_ref[...]
    top = jnp.maximum(jnp.max(table, axis=1, keepdims=True), own[:, 0:1])
    shares = jnp.exp2(table - top)
    own_share = jnp.exp2(own[:, 0:1] - top)
    total = jnp.sum(shares, axis=1, keepdims=True) + own_share
    result = own_share * suffix_ref[...]
    for c in range(sources):
        result += shares[:, c : c + 1] * parts_ref[c, 0:rows, :].astype(F32)
    result_ref[...] = result / total
    group = rows // sessions // heads
    for h in range(heads):
        for g in range(group):
            first = h * sessions * group + g
            piece = result_ref[pl.ds(first, sessions, stride=group), :].astype(BF16)
            column = (h * group + g) * dim
            for copy in range(copies):
                out_ref[copy, :, column : column + dim] = piece


def merge(parts, suffix, suffix_lse, sessions, heads, copies):
    rows, dim = suffix.shape
    return pl.pallas_call(
        functools.partial(merge_kernel, heads),
        scratch_shapes=[pltpu.VMEM((rows, dim), F32)],
        compiler_params=pltpu.CompilerParams(vmem_limit_bytes=16 << 20),
        out_shape=jax.ShapeDtypeStruct((copies, sessions, rows // sessions * dim), BF16),
        name="merge_shards",
    )(parts, suffix, suffix_lse)


def project_kernel(place_ref, attended_ref, *refs):
    weights, out_ref = refs[:-1], refs[-1]
    heads, wide, rows, columns = out_ref.shape
    for k, weight_ref in enumerate(weights):
        product = jnp.dot(attended_ref[...], weight_ref[...], preferred_element_type=F32)
        x = lax.rem(place_ref[0] + (wide - k), wide)
        out_ref[:, x] = product.astype(BF16).reshape(heads, rows, columns)


def project(place, attended, weights, heads):
    sessions, features = attended.shape
    columns = weights[0].shape[1]
    vmem = pl.BlockSpec(memory_space=pltpu.VMEM)
    return pl.pallas_call(
        project_kernel,
        in_specs=[pl.BlockSpec(memory_space=pltpu.SMEM)] + [vmem] * (1 + len(weights)),
        out_specs=vmem,
        out_shape=jax.ShapeDtypeStruct((heads, len(weights), sessions // heads, columns), BF16),
        compiler_params=pltpu.CompilerParams(vmem_limit_bytes=16 << 20),
        name="project",
    )(place, attended, *weights)


def finish_kernel(parts_ref, out_ref):
    for x in range(parts_ref.shape[1]):
        total = parts_ref[0, x].astype(F32)
        for h in range(1, parts_ref.shape[0]):
            total += parts_ref[h, x].astype(F32)
        out_ref[:, x] = total


def finish(parts):
    _, x, outer, sessions, columns = parts.shape
    return pl.pallas_call(
        finish_kernel,
        out_shape=jax.ShapeDtypeStruct((outer, x, sessions, columns), F32),
        compiler_params=pltpu.CompilerParams(vmem_limit_bytes=16 << 20),
        name="sum_heads",
    )(parts)


def spread_kernel(q_ref, out_ref):
    q = q_ref[...]
    for c in range(out_ref.shape[0]):
        out_ref[c] = q


def spread(queries, copies):
    return pl.pallas_call(
        spread_kernel,
        out_shape=jax.ShapeDtypeStruct((copies,) + queries.shape, queries.dtype),
        name="spread_queries",
    )(queries)


def per_device(queries, prefix_keys, prefix_values, suffix_keys, suffix_values, lengths, out_weight):
    sessions, local_heads, dim = queries.shape
    kv_local = prefix_keys.shape[0]
    scale = LOG2E / math.sqrt(dim)
    ctx = lax.axis_size("ctx")
    heads = lax.axis_size("yh") * lax.axis_size("core")
    wide = lax.axis_size("x")
    low = lax.axis_size("yl")

    gathered = lax.all_to_all(spread(queries, ctx), "ctx", 0, 0, tiled=False)
    weights = [out_weight]
    for k in range(1, wide):
        pairs = [(x, (x + k) % wide) for x in range(wide)]
        weights.append(lax.ppermute(out_weight, "x", pairs))

    parts = prefix_attention(gathered, prefix_keys, prefix_values, scale)
    place = lax.axis_index("x").astype(jnp.int32).reshape(1)
    parts, queries, place = lax.optimization_barrier((parts, queries, place))
    parts = lax.all_to_all(parts, "ctx", 0, 0, tiled=True)
    suffix, suffix_lse = suffix_attention(queries, suffix_keys, suffix_values, lengths, scale)

    group = ctx * low
    everyone = merge(parts, suffix, suffix_lse, sessions, kv_local, group)
    everyone, weights, place = lax.optimization_barrier((everyone, weights, place))
    everyone = lax.all_to_all(everyone, ("ctx", "yl"), 0, 0, tiled=True)
    everyone = everyone.reshape(group * sessions, local_heads * dim)
    partial_out = project(place, everyone, weights, heads)
    partial_out = partial_out.reshape(heads * wide, group * sessions // heads, out_weight.shape[1])
    partial_out = lax.all_to_all(partial_out, ("yh", "core", "x"), 0, 0, tiled=True)
    partial_out = partial_out.reshape(heads, wide, group // heads, sessions, out_weight.shape[1])
    return finish(partial_out).reshape(group * sessions * wide // heads, out_weight.shape[1])


def solution(mesh):
    fine = Mesh(mesh.devices.reshape(8, 2, 2, 2, 4), ("ctx", "yh", "core", "yl", "x"))
    both = ("ctx",) + SESS
    return jax.shard_map(
        per_device,
        mesh=fine,
        in_specs=(
            P(both, HEAD, None),
            P(HEAD, "ctx", None),
            P(HEAD, "ctx", None),
            P(both, HEAD, None, None),
            P(both, HEAD, None, None),
            P(both),
            P(HEAD, both),
        ),
        out_specs=P(HEAD, both),
        check_vma=False,
    )
```

```python
import functools
import math

import jax
import jax.numpy as jnp
from jax import lax
from jax.experimental import pallas as pl
from jax.experimental.pallas import tpu as pltpu
from jax.sharding import Mesh
from jax.sharding import PartitionSpec as P

F32 = jnp.float32
BF16 = jnp.bfloat16
LOG2E = 1.4426950408889634
HEAD = ("yh", "core")
SESS = ("yl", "x")
NT = (((1,), (1,)), ((), ()))


TN = (((0,), (0,)), ((), ()))
SAFE_TOTAL = 2.0**100


def prefix_kernel(
    scale, tile, first, all_q_ref, k_first, v_first, k_hbm, v_hbm, o_ref, q_ref, k_ref, v_ref, acc_ref, top_ref,
    total_ref, lse_ref, k_sem, v_sem,
):
    head = pl.program_id(0)
    sources, sessions, local_heads, dim = all_q_ref.shape
    heads, length, _ = k_ref.shape
    group = local_heads // heads
    rows = sessions * group
    parts = [(tile, first - tile), (first, length - first)]

    def copy_of(source, target, sem, h, part):
        span = pl.ds(*parts[part])
        return pltpu.make_async_copy(source.at[h, span], target.at[h, span], sem.at[h, part])

    @pl.when(head == 0)
    def _():
        for h in range(heads):
            for part in range(len(parts)):
                copy_of(k_hbm, k_ref, k_sem, h, part).start()
                copy_of(v_hbm, v_ref, v_sem, h, part).start()
        for h in range(heads):
            part = all_q_ref[:, :, h * group : (h + 1) * group, :]
            q_ref[h] = part.reshape(sources * rows, dim)

    def scores_of(start, keys=None):
        if keys is None:
            keys = k_ref[head, pl.ds(start, tile), :]
        return lax.dot_general(keys, q_ref[head], NT, preferred_element_type=F32)

    def product_of(weights, start, values=None):
        if values is None:
            values = v_ref[head, pl.ds(start, tile), :]
        return lax.dot_general(values, weights.astype(BF16), TN, preferred_element_type=F32)

    scores = scores_of(0, k_first[head])
    top = jnp.max(scores, axis=0, keepdims=True)
    for start in range(0, length, tile):
        if start == 0:
            copy_of(k_hbm, k_ref, k_sem, head, 0).wait()
        if start == tile:
            copy_of(v_hbm, v_ref, v_sem, head, 0).wait()
        if start == first:
            copy_of(v_hbm, v_ref, v_sem, head, 1).wait()
        if start + tile == first:
            copy_of(k_hbm, k_ref, k_sem, head, 1).wait()
        ahead = scores_of(start + tile) if start + tile < length else None
        weights = jnp.exp2((scores - top) * scale)
        share = jnp.sum(weights, axis=0, keepdims=True)
        product = product_of(weights, start, v_first[head] if start == 0 else None)
        if start == 0:
            total = share
            acc_ref[...] = product
        else:
            total = total + share
            acc_ref[...] = acc_ref[...] + product
        scores = ahead
    top_ref[...] = top
    total_ref[...] = total

    unsafe = jnp.max(jnp.where(total <= SAFE_TOTAL, 0.0, 1.0))

    @pl.when(unsafe > 0.0)
    def _():
        top_ref[...] = jnp.full_like(top_ref, -1e30)
        total_ref[...] = jnp.zeros_like(total_ref)
        acc_ref[...] = jnp.zeros_like(acc_ref)
        k_ref[head, :tile] = k_first[head]
        v_ref[head, :tile] = v_first[head]

        def step(index, carry):
            start = pl.multiple_of(index * tile, tile)
            scores = scores_of(start)
            old = top_ref[...]
            new = jnp.maximum(old, jnp.max(scores, axis=0, keepdims=True))
            factor = jnp.exp2((old - new) * scale)
            weights = jnp.exp2((scores - new) * scale)
            total_ref[...] = total_ref[...] * factor + jnp.sum(weights, axis=0, keepdims=True)
            acc_ref[...] = acc_ref[...] * factor + product_of(weights, start)
            top_ref[...] = new
            return carry

        lax.fori_loop(0, length // tile, step, 0)

    out = (acc_ref[...] / total_ref[...]).T.astype(BF16)
    lse_ref[head] = jnp.broadcast_to(
        top_ref[...] * scale + jnp.log2(total_ref[...]), lse_ref.shape[1:]
    )
    for c in range(sources):
        o_ref[c, pl.ds(head * rows, rows), :] = out[c * rows : (c + 1) * rows]

    @pl.when(head == heads - 1)
    def _():
        for c in range(sources):
            row = jnp.concatenate(
                [lse_ref[h, :, c * rows : (c + 1) * rows] for h in range(heads)], axis=1
            )
            high = row.astype(BF16).astype(F32)
            middle = (row - high).astype(BF16).astype(F32)
            low = row - high - middle
            place = lax.broadcasted_iota(jnp.int32, row.shape, 0)
            stats = jnp.where(place == 0, high, jnp.where(place == 1, middle, low))
            o_ref[c, heads * rows : heads * rows + 8, :] = stats.astype(BF16)


def prefix_attention(q, k_first, v_first, keys, values, scale):
    sources, sessions, local_heads, dim = q.shape
    heads, length, _ = keys.shape
    rows = sessions * local_heads // heads
    total_rows = sources * rows
    return pl.pallas_call(
        functools.partial(prefix_kernel, scale, k_first.shape[1], 2 * k_first.shape[1]),
        grid=(heads,),
        in_specs=[
            pl.BlockSpec(q.shape, lambda h: (0, 0, 0, 0)),
            pl.BlockSpec(k_first.shape, lambda h: (0, 0, 0)),
            pl.BlockSpec(v_first.shape, lambda h: (0, 0, 0)),
            pl.BlockSpec(memory_space=pltpu.HBM),
            pl.BlockSpec(memory_space=pltpu.HBM),
        ],
        out_specs=pl.BlockSpec((sources, heads * rows + 8, dim), lambda h: (0, 0, 0)),
        out_shape=jax.ShapeDtypeStruct((sources, heads * rows + 8, dim), BF16),
        scratch_shapes=[
            pltpu.VMEM((heads, total_rows, dim), BF16),
            pltpu.VMEM(keys.shape, BF16),
            pltpu.VMEM(values.shape, BF16),
            pltpu.VMEM((dim, total_rows), F32),
            pltpu.VMEM((1, total_rows), F32),
            pltpu.VMEM((1, total_rows), F32),
            pltpu.VMEM((heads, 8, total_rows), F32),
            pltpu.SemaphoreType.DMA((heads, 2)),
            pltpu.SemaphoreType.DMA((heads, 2)),
        ],
        compiler_params=pltpu.CompilerParams(
            dimension_semantics=("arbitrary",), vmem_limit_bytes=32 << 20
        ),
        cost_estimate=pl.CostEstimate(
            flops=4 * heads * total_rows * length * dim,
            bytes_accessed=4 * heads * length * dim,
            transcendentals=heads * total_rows * length,
        ),
        name="prefix_attention",
    )(
        q,
        k_first,
        v_first,
        pltpu.with_memory_space_constraint(keys, pltpu.HBM),
        pltpu.with_memory_space_constraint(values, pltpu.HBM),
    )


def suffix_kernel(scale, lengths_ref, q_ref, k_ref, v_ref, o_ref, lse_ref):
    step = pl.program_id(0)
    count, heads, length = k_ref.shape[0], k_ref.shape[1], k_ref.shape[2]
    group = q_ref.shape[1] // heads
    sessions = pl.num_programs(0) * count
    pairs = [(s, h) for s in range(count) for h in range(heads)]
    all_scores = [
        lax.dot_general(
            q_ref[s, h * group : (h + 1) * group], k_ref[s, h], NT, preferred_element_type=F32
        )
        for s, h in pairs
    ]
    position = lax.broadcasted_iota(jnp.int32, (group, length), 1)
    softened = []
    for (s, h), scores in zip(pairs, all_scores):
        scores = jnp.where(position < lengths_ref[step * count + s], scores, -1e30)
        top = jnp.max(scores, axis=1, keepdims=True)
        weights = jnp.exp2((scores - top) * scale)
        softened.append((top, jnp.sum(weights, axis=1, keepdims=True), weights.astype(BF16)))
    for (s, h), (top, total, weights) in zip(pairs, softened):
        out = jnp.dot(weights, v_ref[s, h], preferred_element_type=F32) / total
        rows = pl.ds((h * sessions + step * count + s) * group, group)
        o_ref[rows, :] = out
        lse_ref[rows, :] = jnp.broadcast_to(top * scale + jnp.log2(total), out.shape)


def suffix_attention(q, keys, values, lengths, scale):
    sessions, heads, length, dim = keys.shape
    rows = q.shape[1] * sessions
    count = 4
    spec = pl.BlockSpec((rows, dim), lambda s, n: (0, 0))
    return pl.pallas_call(
        functools.partial(suffix_kernel, scale),
        grid_spec=pltpu.PrefetchScalarGridSpec(
            num_scalar_prefetch=1,
            grid=(sessions // count,),
            in_specs=[
                pl.BlockSpec((count,) + q.shape[1:], lambda s, n: (s, 0, 0)),
                pl.BlockSpec((count, heads, length, dim), lambda s, n: (s, 0, 0, 0)),
                pl.BlockSpec((count, heads, length, dim), lambda s, n: (s, 0, 0, 0)),
            ],
            out_specs=[spec, spec],
        ),
        out_shape=[jax.ShapeDtypeStruct((rows, dim), F32)] * 2,
        compiler_params=pltpu.CompilerParams(vmem_limit_bytes=16 << 20),
        cost_estimate=pl.CostEstimate(
            flops=4 * rows * length * dim,
            bytes_accessed=4 * sessions * heads * length * dim,
            transcendentals=rows * length,
        ),
        name="suffix_attention",
    )(
        lengths,
        q,
        pltpu.with_memory_space_constraint(keys, pltpu.HBM),
        pltpu.with_memory_space_constraint(values, pltpu.HBM),
    )


def merge_kernel(heads, parts_ref, suffix_ref, suffix_lse_ref, out_ref, result_ref):
    sources, padded, dim = parts_ref.shape
    rows = padded - 8
    copies, sessions, _ = out_ref.shape
    stats = []
    for c in range(sources):
        three = parts_ref[c, rows : rows + 8, :].astype(F32)
        stats.append(three[0:1] + three[1:2] + three[2:3])
    filler = jnp.full((rows - sources, rows), -3e38, F32)
    table = jnp.concatenate(stats + [filler], axis=0).T
    own = suffix_lse_ref[...]
    top = jnp.maximum(jnp.max(table, axis=1, keepdims=True), own[:, 0:1])
    shares = jnp.exp2(table - top)
    own_share = jnp.exp2(own[:, 0:1] - top)
    total = jnp.sum(shares, axis=1, keepdims=True) + own_share
    result = own_share * suffix_ref[...]
    for c in range(sources):
        result += shares[:, c : c + 1] * parts_ref[c, 0:rows, :].astype(F32)
    result_ref[...] = result / total
    group = rows // sessions // heads
    for h in range(heads):
        for g in range(group):
            first = h * sessions * group + g
            piece = result_ref[pl.ds(first, sessions, stride=group), :].astype(BF16)
            column = (h * group + g) * dim
            for copy in range(copies):
                out_ref[copy, :, column : column + dim] = piece


def merge(parts, suffix, suffix_lse, sessions, heads, copies):
    rows, dim = suffix.shape
    return pl.pallas_call(
        functools.partial(merge_kernel, heads),
        scratch_shapes=[pltpu.VMEM((rows, dim), F32)],
        compiler_params=pltpu.CompilerParams(vmem_limit_bytes=16 << 20),
        out_shape=jax.ShapeDtypeStruct((copies, sessions, rows // sessions * dim), BF16),
        name="merge_shards",
    )(parts, suffix, suffix_lse)


def project_kernel(place_ref, attended_ref, *refs):
    weights, out_ref = refs[:-1], refs[-1]
    heads, wide, rows, columns = out_ref.shape
    for k, weight_ref in enumerate(weights):
        product = jnp.dot(attended_ref[...], weight_ref[...], preferred_element_type=F32)
        x = lax.rem(place_ref[0] + (wide - k), wide)
        out_ref[:, x] = product.astype(BF16).reshape(heads, rows, columns)


def project(place, attended, weights, heads):
    sessions, features = attended.shape
    columns = weights[0].shape[1]
    vmem = pl.BlockSpec(memory_space=pltpu.VMEM)
    return pl.pallas_call(
        project_kernel,
        in_specs=[pl.BlockSpec(memory_space=pltpu.SMEM)] + [vmem] * (1 + len(weights)),
        out_specs=vmem,
        out_shape=jax.ShapeDtypeStruct((heads, len(weights), sessions // heads, columns), BF16),
        compiler_params=pltpu.CompilerParams(vmem_limit_bytes=16 << 20),
        name="project",
    )(place, attended, *weights)


def finish_kernel(parts_ref, out_ref):
    for x in range(parts_ref.shape[1]):
        total = parts_ref[0, x].astype(F32)
        for h in range(1, parts_ref.shape[0]):
            total += parts_ref[h, x].astype(F32)
        out_ref[:, x] = total


def finish(parts):
    _, x, outer, sessions, columns = parts.shape
    return pl.pallas_call(
        finish_kernel,
        out_shape=jax.ShapeDtypeStruct((outer, x, sessions, columns), F32),
        compiler_params=pltpu.CompilerParams(vmem_limit_bytes=16 << 20),
        name="sum_heads",
    )(parts)


def spread_kernel(q_ref, out_ref, sem):
    copies = [
        pltpu.make_async_copy(q_ref, out_ref.at[c], sem.at[c]) for c in range(out_ref.shape[0])
    ]
    for copy in copies:
        copy.start()
    for copy in copies:
        copy.wait()


def spread(queries, copies):
    return pl.pallas_call(
        spread_kernel,
        in_specs=[pl.BlockSpec(memory_space=pltpu.VMEM)],
        out_specs=pl.BlockSpec(memory_space=pl.ANY),
        out_shape=jax.ShapeDtypeStruct((copies,) + queries.shape, queries.dtype),
        scratch_shapes=[pltpu.SemaphoreType.DMA((copies,))],
        name="spread_queries",
    )(queries)


def per_device(queries, prefix_keys, prefix_values, suffix_keys, suffix_values, lengths, out_weight):
    sessions, local_heads, dim = queries.shape
    kv_local = prefix_keys.shape[0]
    scale = LOG2E / math.sqrt(dim)
    ctx = lax.axis_size("ctx")
    heads = lax.axis_size("yh") * lax.axis_size("core")
    wide = lax.axis_size("x")
    low = lax.axis_size("yl")

    gathered = lax.all_to_all(spread(queries, ctx), "ctx", 0, 0, tiled=False)
    weights = [out_weight]
    for k in range(1, wide):
        pairs = [(x, (x + k) % wide) for x in range(wide)]
        weights.append(lax.ppermute(out_weight, "x", pairs))

    tile = prefix_keys.shape[1] // 12
    k_first, v_first = prefix_keys[:, :tile], prefix_values[:, :tile]
    parts = prefix_attention(gathered, k_first, v_first, prefix_keys, prefix_values, scale)
    place = lax.axis_index("x").astype(jnp.int32).reshape(1)
    parts, queries, place = lax.optimization_barrier((parts, queries, place))
    parts = lax.all_to_all(parts, "ctx", 0, 0, tiled=True)
    suffix, suffix_lse = suffix_attention(queries, suffix_keys, suffix_values, lengths, scale)

    group = ctx * low
    everyone = merge(parts, suffix, suffix_lse, sessions, kv_local, group)
    everyone, weights, place = lax.optimization_barrier((everyone, weights, place))
    everyone = lax.all_to_all(everyone, ("ctx", "yl"), 0, 0, tiled=True)
    everyone = everyone.reshape(group * sessions, local_heads * dim)
    partial_out = project(place, everyone, weights, heads)
    partial_out = partial_out.reshape(heads * wide, group * sessions // heads, out_weight.shape[1])
    partial_out = lax.all_to_all(partial_out, ("yh", "core", "x"), 0, 0, tiled=True)
    partial_out = partial_out.reshape(heads, wide, group // heads, sessions, out_weight.shape[1])
    return finish(partial_out).reshape(group * sessions * wide // heads, out_weight.shape[1])


def solution(mesh):
    fine = Mesh(mesh.devices.reshape(8, 2, 2, 2, 4), ("ctx", "yh", "core", "yl", "x"))
    both = ("ctx",) + SESS
    return jax.shard_map(
        per_device,
        mesh=fine,
        in_specs=(
            P(both, HEAD, None),
            P(HEAD, "ctx", None),
            P(HEAD, "ctx", None),
            P(both, HEAD, None, None),
            P(both, HEAD, None, None),
            P(both),
            P(HEAD, both),
        ),
        out_specs=P(HEAD, both),
        check_vma=False,
    )
```

```python
import functools
import math

import jax
import jax.numpy as jnp
from jax import lax
from jax.experimental import pallas as pl
from jax.experimental.pallas import tpu as pltpu
from jax.sharding import Mesh
from jax.sharding import PartitionSpec as P

F32 = jnp.float32
BF16 = jnp.bfloat16
LOG2E = 1.4426950408889634
HEAD = ("yh", "core")
SESS = ("yl", "x")
NT = (((1,), (1,)), ((), ()))


TN = (((0,), (0,)), ((), ()))
SAFE_TOTAL = 2.0**100


def prefix_kernel(
    scale, tile, first, q_ref, k_first, v_first, k_hbm, v_hbm, o_ref, k_ref, v_ref, acc_ref, top_ref,
    total_ref, lse_ref, k_sem, v_sem,
):
    head = pl.program_id(0)
    sources, _, rows, dim = q_ref.shape
    heads, length, _ = k_ref.shape
    parts = [(tile, first - tile), (first, length - first)]

    def copy_of(source, target, sem, h, part):
        span = pl.ds(*parts[part])
        return pltpu.make_async_copy(source.at[h, span], target.at[h, span], sem.at[h, part])

    @pl.when(head == 0)
    def _():
        for h in range(heads):
            for part in range(len(parts)):
                copy_of(k_hbm, k_ref, k_sem, h, part).start()
                copy_of(v_hbm, v_ref, v_sem, h, part).start()

    queries = q_ref[...].reshape(sources * rows, dim)

    def scores_of(start, keys=None):
        if keys is None:
            keys = k_ref[head, pl.ds(start, tile), :]
        return lax.dot_general(keys, queries, NT, preferred_element_type=F32)

    def product_of(weights, start, values=None):
        if values is None:
            values = v_ref[head, pl.ds(start, tile), :]
        return lax.dot_general(values, weights.astype(BF16), TN, preferred_element_type=F32)

    scores = scores_of(0, k_first[head])
    top = jnp.max(scores, axis=0, keepdims=True)
    for start in range(0, length, tile):
        if start == 0:
            copy_of(k_hbm, k_ref, k_sem, head, 0).wait()
        if start == tile:
            copy_of(v_hbm, v_ref, v_sem, head, 0).wait()
        if start == first:
            copy_of(v_hbm, v_ref, v_sem, head, 1).wait()
        if start + tile == first:
            copy_of(k_hbm, k_ref, k_sem, head, 1).wait()
        ahead = scores_of(start + tile) if start + tile < length else None
        weights = jnp.exp2((scores - top) * scale)
        share = jnp.sum(weights, axis=0, keepdims=True)
        product = product_of(weights, start, v_first[head] if start == 0 else None)
        if start == 0:
            total = share
            acc_ref[...] = product
        else:
            total = total + share
            acc_ref[...] = acc_ref[...] + product
        scores = ahead
    top_ref[...] = top
    total_ref[...] = total

    unsafe = jnp.max(jnp.where(total <= SAFE_TOTAL, 0.0, 1.0))

    @pl.when(unsafe > 0.0)
    def _():
        top_ref[...] = jnp.full_like(top_ref, -1e30)
        total_ref[...] = jnp.zeros_like(total_ref)
        acc_ref[...] = jnp.zeros_like(acc_ref)
        k_ref[head, :tile] = k_first[head]
        v_ref[head, :tile] = v_first[head]

        def step(index, carry):
            start = pl.multiple_of(index * tile, tile)
            scores = scores_of(start)
            old = top_ref[...]
            new = jnp.maximum(old, jnp.max(scores, axis=0, keepdims=True))
            factor = jnp.exp2((old - new) * scale)
            weights = jnp.exp2((scores - new) * scale)
            total_ref[...] = total_ref[...] * factor + jnp.sum(weights, axis=0, keepdims=True)
            acc_ref[...] = acc_ref[...] * factor + product_of(weights, start)
            top_ref[...] = new
            return carry

        lax.fori_loop(0, length // tile, step, 0)

    out = (acc_ref[...] / total_ref[...]).T.astype(BF16)
    lse_ref[head] = jnp.broadcast_to(
        top_ref[...] * scale + jnp.log2(total_ref[...]), lse_ref.shape[1:]
    )
    for c in range(sources):
        o_ref[c, pl.ds(head * rows, rows), :] = out[c * rows : (c + 1) * rows]

    @pl.when(head == heads - 1)
    def _():
        for c in range(sources):
            row = jnp.concatenate(
                [lse_ref[h, :, c * rows : (c + 1) * rows] for h in range(heads)], axis=1
            )
            high = row.astype(BF16).astype(F32)
            middle = (row - high).astype(BF16).astype(F32)
            low = row - high - middle
            place = lax.broadcasted_iota(jnp.int32, row.shape, 0)
            stats = jnp.where(place == 0, high, jnp.where(place == 1, middle, low))
            o_ref[c, heads * rows : heads * rows + 8, :] = stats.astype(BF16)


def prefix_attention(q, k_first, v_first, keys, values, scale):
    sources, heads, rows, dim = q.shape
    length = keys.shape[1]
    total_rows = sources * rows
    return pl.pallas_call(
        functools.partial(prefix_kernel, scale, k_first.shape[1], 2 * k_first.shape[1]),
        grid=(heads,),
        in_specs=[
            pl.BlockSpec((sources, 1, rows, dim), lambda h: (0, h, 0, 0)),
            pl.BlockSpec(k_first.shape, lambda h: (0, 0, 0)),
            pl.BlockSpec(v_first.shape, lambda h: (0, 0, 0)),
            pl.BlockSpec(memory_space=pltpu.HBM),
            pl.BlockSpec(memory_space=pltpu.HBM),
        ],
        out_specs=pl.BlockSpec((sources, heads * rows + 8, dim), lambda h: (0, 0, 0)),
        out_shape=jax.ShapeDtypeStruct((sources, heads * rows + 8, dim), BF16),
        scratch_shapes=[
            pltpu.VMEM(keys.shape, BF16),
            pltpu.VMEM(values.shape, BF16),
            pltpu.VMEM((dim, total_rows), F32),
            pltpu.VMEM((1, total_rows), F32),
            pltpu.VMEM((1, total_rows), F32),
            pltpu.VMEM((heads, 8, total_rows), F32),
            pltpu.SemaphoreType.DMA((heads, 2)),
            pltpu.SemaphoreType.DMA((heads, 2)),
        ],
        compiler_params=pltpu.CompilerParams(
            dimension_semantics=("arbitrary",), vmem_limit_bytes=32 << 20
        ),
        cost_estimate=pl.CostEstimate(
            flops=4 * heads * total_rows * length * dim,
            bytes_accessed=4 * heads * length * dim,
            transcendentals=heads * total_rows * length,
        ),
        name="prefix_attention",
    )(
        q,
        k_first,
        v_first,
        pltpu.with_memory_space_constraint(keys, pltpu.HBM),
        pltpu.with_memory_space_constraint(values, pltpu.HBM),
    )


def suffix_kernel(scale, lengths_ref, q_ref, k_ref, v_ref, o_ref, lse_ref):
    step = pl.program_id(0)
    count, heads, length = k_ref.shape[0], k_ref.shape[1], k_ref.shape[2]
    group = q_ref.shape[1] // heads
    sessions = pl.num_programs(0) * count
    pairs = [(s, h) for s in range(count) for h in range(heads)]
    all_scores = [
        lax.dot_general(
            q_ref[s, h * group : (h + 1) * group], k_ref[s, h], NT, preferred_element_type=F32
        )
        for s, h in pairs
    ]
    position = lax.broadcasted_iota(jnp.int32, (group, length), 1)
    softened = []
    for (s, h), scores in zip(pairs, all_scores):
        scores = jnp.where(position < lengths_ref[step * count + s], scores, -1e30)
        top = jnp.max(scores, axis=1, keepdims=True)
        weights = jnp.exp2((scores - top) * scale)
        softened.append((top, jnp.sum(weights, axis=1, keepdims=True), weights.astype(BF16)))
    for (s, h), (top, total, weights) in zip(pairs, softened):
        out = jnp.dot(weights, v_ref[s, h], preferred_element_type=F32) / total
        rows = pl.ds((h * sessions + step * count + s) * group, group)
        o_ref[rows, :] = out
        lse_ref[rows, :] = jnp.broadcast_to(top * scale + jnp.log2(total), out.shape)


def suffix_attention(q, keys, values, lengths, scale):
    sessions, heads, length, dim = keys.shape
    rows = q.shape[1] * sessions
    count = 4
    spec = pl.BlockSpec((rows, dim), lambda s, n: (0, 0))
    return pl.pallas_call(
        functools.partial(suffix_kernel, scale),
        grid_spec=pltpu.PrefetchScalarGridSpec(
            num_scalar_prefetch=1,
            grid=(sessions // count,),
            in_specs=[
                pl.BlockSpec((count,) + q.shape[1:], lambda s, n: (s, 0, 0)),
                pl.BlockSpec((count, heads, length, dim), lambda s, n: (s, 0, 0, 0)),
                pl.BlockSpec((count, heads, length, dim), lambda s, n: (s, 0, 0, 0)),
            ],
            out_specs=[spec, spec],
        ),
        out_shape=[jax.ShapeDtypeStruct((rows, dim), F32)] * 2,
        compiler_params=pltpu.CompilerParams(vmem_limit_bytes=16 << 20),
        cost_estimate=pl.CostEstimate(
            flops=4 * rows * length * dim,
            bytes_accessed=4 * sessions * heads * length * dim,
            transcendentals=rows * length,
        ),
        name="suffix_attention",
    )(
        lengths,
        q,
        pltpu.with_memory_space_constraint(keys, pltpu.HBM),
        pltpu.with_memory_space_constraint(values, pltpu.HBM),
    )


def merge_kernel(heads, parts_ref, suffix_ref, suffix_lse_ref, out_ref, result_ref):
    sources, padded, dim = parts_ref.shape
    rows = padded - 8
    copies, sessions, _ = out_ref.shape
    stats = []
    for c in range(sources):
        three = parts_ref[c, rows : rows + 8, :].astype(F32)
        stats.append(three[0:1] + three[1:2] + three[2:3])
    filler = jnp.full((rows - sources, rows), -3e38, F32)
    table = jnp.concatenate(stats + [filler], axis=0).T
    own = suffix_lse_ref[...]
    top = jnp.maximum(jnp.max(table, axis=1, keepdims=True), own[:, 0:1])
    shares = jnp.exp2(table - top)
    own_share = jnp.exp2(own[:, 0:1] - top)
    total = jnp.sum(shares, axis=1, keepdims=True) + own_share
    result = own_share * suffix_ref[...]
    for c in range(sources):
        result += shares[:, c : c + 1] * parts_ref[c, 0:rows, :].astype(F32)
    result_ref[...] = result / total
    group = rows // sessions // heads
    for h in range(heads):
        for g in range(group):
            first = h * sessions * group + g
            piece = result_ref[pl.ds(first, sessions, stride=group), :].astype(BF16)
            column = (h * group + g) * dim
            for copy in range(copies):
                out_ref[copy, :, column : column + dim] = piece


def merge(parts, suffix, suffix_lse, sessions, heads, copies):
    rows, dim = suffix.shape
    return pl.pallas_call(
        functools.partial(merge_kernel, heads),
        scratch_shapes=[pltpu.VMEM((rows, dim), F32)],
        compiler_params=pltpu.CompilerParams(vmem_limit_bytes=16 << 20),
        out_shape=jax.ShapeDtypeStruct((copies, sessions, rows // sessions * dim), BF16),
        name="merge_shards",
    )(parts, suffix, suffix_lse)


def project_kernel(place_ref, attended_ref, *refs):
    weights, out_ref = refs[:-1], refs[-1]
    heads, wide, rows, columns = out_ref.shape
    for k, weight_ref in enumerate(weights):
        product = jnp.dot(attended_ref[...], weight_ref[...], preferred_element_type=F32)
        x = lax.rem(place_ref[0] + (wide - k), wide)
        out_ref[:, x] = product.astype(BF16).reshape(heads, rows, columns)


def project(place, attended, weights, heads):
    sessions, features = attended.shape
    columns = weights[0].shape[1]
    vmem = pl.BlockSpec(memory_space=pltpu.VMEM)
    return pl.pallas_call(
        project_kernel,
        in_specs=[pl.BlockSpec(memory_space=pltpu.SMEM)] + [vmem] * (1 + len(weights)),
        out_specs=vmem,
        out_shape=jax.ShapeDtypeStruct((heads, len(weights), sessions // heads, columns), BF16),
        compiler_params=pltpu.CompilerParams(vmem_limit_bytes=16 << 20),
        name="project",
    )(place, attended, *weights)


def finish_kernel(parts_ref, out_ref):
    for x in range(parts_ref.shape[1]):
        total = parts_ref[0, x].astype(F32)
        for h in range(1, parts_ref.shape[0]):
            total += parts_ref[h, x].astype(F32)
        out_ref[:, x] = total


def finish(parts):
    _, x, outer, sessions, columns = parts.shape
    return pl.pallas_call(
        finish_kernel,
        out_shape=jax.ShapeDtypeStruct((outer, x, sessions, columns), F32),
        compiler_params=pltpu.CompilerParams(vmem_limit_bytes=16 << 20),
        name="sum_heads",
    )(parts)


def spread_kernel(q_ref, out_ref):
    copies, heads, rows, dim = out_ref.shape
    group = q_ref.shape[1] // heads
    for h in range(heads):
        q = q_ref[:, h * group : (h + 1) * group, :].reshape(rows, dim)
        for c in range(copies):
            out_ref[c, h] = q


def spread(queries, copies, heads):
    sessions, local_heads, dim = queries.shape
    shape = (copies, heads, sessions * local_heads // heads, dim)
    return pl.pallas_call(
        spread_kernel,
        out_shape=jax.ShapeDtypeStruct(shape, queries.dtype),
        name="spread_queries",
    )(queries)


def per_device(queries, prefix_keys, prefix_values, suffix_keys, suffix_values, lengths, out_weight):
    sessions, local_heads, dim = queries.shape
    kv_local = prefix_keys.shape[0]
    scale = LOG2E / math.sqrt(dim)
    ctx = lax.axis_size("ctx")
    heads = lax.axis_size("yh") * lax.axis_size("core")
    wide = lax.axis_size("x")
    low = lax.axis_size("yl")

    gathered = lax.all_to_all(spread(queries, ctx, kv_local), "ctx", 0, 0, tiled=False)
    weights = [out_weight]
    for k in range(1, wide):
        pairs = [(x, (x + k) % wide) for x in range(wide)]
        weights.append(lax.ppermute(out_weight, "x", pairs))

    tile = prefix_keys.shape[1] // 12
    k_first, v_first = prefix_keys[:, :tile], prefix_values[:, :tile]
    parts = prefix_attention(gathered, k_first, v_first, prefix_keys, prefix_values, scale)
    place = lax.axis_index("x").astype(jnp.int32).reshape(1)
    parts, queries, place = lax.optimization_barrier((parts, queries, place))
    parts = lax.all_to_all(parts, "ctx", 0, 0, tiled=True)
    suffix, suffix_lse = suffix_attention(queries, suffix_keys, suffix_values, lengths, scale)

    group = ctx * low
    everyone = merge(parts, suffix, suffix_lse, sessions, kv_local, group)
    everyone, weights, place = lax.optimization_barrier((everyone, weights, place))
    everyone = lax.all_to_all(everyone, ("ctx", "yl"), 0, 0, tiled=True)
    everyone = everyone.reshape(group * sessions, local_heads * dim)
    partial_out = project(place, everyone, weights, heads)
    partial_out = partial_out.reshape(heads * wide, group * sessions // heads, out_weight.shape[1])
    partial_out = lax.all_to_all(partial_out, ("yh", "core", "x"), 0, 0, tiled=True)
    partial_out = partial_out.reshape(heads, wide, group // heads, sessions, out_weight.shape[1])
    return finish(partial_out).reshape(group * sessions * wide // heads, out_weight.shape[1])


def solution(mesh):
    fine = Mesh(mesh.devices.reshape(8, 2, 2, 2, 4), ("ctx", "yh", "core", "yl", "x"))
    both = ("ctx",) + SESS
    return jax.shard_map(
        per_device,
        mesh=fine,
        in_specs=(
            P(both, HEAD, None),
            P(HEAD, "ctx", None),
            P(HEAD, "ctx", None),
            P(both, HEAD, None, None),
            P(both, HEAD, None, None),
            P(both),
            P(HEAD, both),
        ),
        out_specs=P(HEAD, both),
        check_vma=False,
    )
```

```python
import functools
import math

import jax
import jax.numpy as jnp
from jax import lax
from jax.experimental import pallas as pl
from jax.experimental.pallas import tpu as pltpu
from jax.sharding import Mesh
from jax.sharding import PartitionSpec as P

F32 = jnp.float32
BF16 = jnp.bfloat16
LOG2E = 1.4426950408889634
HEAD = ("yh", "core")
SESS = ("yl", "x")
NT = (((1,), (1,)), ((), ()))


TN = (((0,), (0,)), ((), ()))
SAFE_TOTAL = 2.0**100


def prefix_kernel(
    scale, tile, first, q_ref, k_hbm, v_hbm, o_ref, k_ref, v_ref, acc_ref, top_ref,
    total_ref, lse_ref, k_sem, v_sem,
):
    head = pl.program_id(0)
    sources, _, rows, dim = q_ref.shape
    heads, length, _ = k_ref.shape
    parts = [(0, first), (first, length - first)]

    def copy_of(source, target, sem, h, part):
        span = pl.ds(*parts[part])
        return pltpu.make_async_copy(source.at[h, span], target.at[h, span], sem.at[h, part])

    @pl.when(head == 0)
    def _():
        for h in range(heads):
            for part in range(len(parts)):
                copy_of(k_hbm, k_ref, k_sem, h, part).start()
                copy_of(v_hbm, v_ref, v_sem, h, part).start()

    queries = q_ref[...].reshape(sources * rows, dim)

    def scores_of(start):
        keys = k_ref[head, pl.ds(start, tile), :]
        return lax.dot_general(keys, queries, NT, preferred_element_type=F32)

    def product_of(weights, start):
        values = v_ref[head, pl.ds(start, tile), :]
        return lax.dot_general(values, weights.astype(BF16), TN, preferred_element_type=F32)

    copy_of(k_hbm, k_ref, k_sem, head, 0).wait()
    scores = scores_of(0)
    top = jnp.max(scores, axis=0, keepdims=True)
    for start in range(0, length, tile):
        if start == 0:
            copy_of(v_hbm, v_ref, v_sem, head, 0).wait()
        if start == first:
            copy_of(v_hbm, v_ref, v_sem, head, 1).wait()
        if start + tile == first:
            copy_of(k_hbm, k_ref, k_sem, head, 1).wait()
        ahead = scores_of(start + tile) if start + tile < length else None
        weights = jnp.exp2((scores - top) * scale)
        share = jnp.sum(weights, axis=0, keepdims=True)
        product = product_of(weights, start)
        if start == 0:
            total = share
            acc_ref[...] = product
        else:
            total = total + share
            acc_ref[...] = acc_ref[...] + product
        scores = ahead
    top_ref[...] = top
    total_ref[...] = total

    unsafe = jnp.max(jnp.where(total <= SAFE_TOTAL, 0.0, 1.0))

    @pl.when(unsafe > 0.0)
    def _():
        top_ref[...] = jnp.full_like(top_ref, -1e30)
        total_ref[...] = jnp.zeros_like(total_ref)
        acc_ref[...] = jnp.zeros_like(acc_ref)

        def step(index, carry):
            start = pl.multiple_of(index * tile, tile)
            scores = scores_of(start)
            old = top_ref[...]
            new = jnp.maximum(old, jnp.max(scores, axis=0, keepdims=True))
            factor = jnp.exp2((old - new) * scale)
            weights = jnp.exp2((scores - new) * scale)
            total_ref[...] = total_ref[...] * factor + jnp.sum(weights, axis=0, keepdims=True)
            acc_ref[...] = acc_ref[...] * factor + product_of(weights, start)
            top_ref[...] = new
            return carry

        lax.fori_loop(0, length // tile, step, 0)

    out = (acc_ref[...] / total_ref[...]).T.astype(BF16)
    lse_ref[head] = jnp.broadcast_to(
        top_ref[...] * scale + jnp.log2(total_ref[...]), lse_ref.shape[1:]
    )
    for c in range(sources):
        o_ref[c, pl.ds(head * rows, rows), :] = out[c * rows : (c + 1) * rows]

    @pl.when(head == heads - 1)
    def _():
        for c in range(sources):
            row = jnp.concatenate(
                [lse_ref[h, :, c * rows : (c + 1) * rows] for h in range(heads)], axis=1
            )
            high = row.astype(BF16).astype(F32)
            middle = (row - high).astype(BF16).astype(F32)
            low = row - high - middle
            place = lax.broadcasted_iota(jnp.int32, row.shape, 0)
            stats = jnp.where(place == 0, high, jnp.where(place == 1, middle, low))
            o_ref[c, heads * rows : heads * rows + 8, :] = stats.astype(BF16)


def prefix_attention(q, keys, values, scale):
    sources, heads, rows, dim = q.shape
    length = keys.shape[1]
    total_rows = sources * rows
    return pl.pallas_call(
        functools.partial(prefix_kernel, scale, length // 12, length // 6),
        grid=(heads,),
        in_specs=[
            pl.BlockSpec((sources, 1, rows, dim), lambda h: (0, h, 0, 0)),
            pl.BlockSpec(memory_space=pltpu.HBM),
            pl.BlockSpec(memory_space=pltpu.HBM),
        ],
        out_specs=pl.BlockSpec((sources, heads * rows + 8, dim), lambda h: (0, 0, 0)),
        out_shape=jax.ShapeDtypeStruct((sources, heads * rows + 8, dim), BF16),
        scratch_shapes=[
            pltpu.VMEM(keys.shape, BF16),
            pltpu.VMEM(values.shape, BF16),
            pltpu.VMEM((dim, total_rows), F32),
            pltpu.VMEM((1, total_rows), F32),
            pltpu.VMEM((1, total_rows), F32),
            pltpu.VMEM((heads, 8, total_rows), F32),
            pltpu.SemaphoreType.DMA((heads, 2)),
            pltpu.SemaphoreType.DMA((heads, 2)),
        ],
        compiler_params=pltpu.CompilerParams(
            dimension_semantics=("arbitrary",), vmem_limit_bytes=32 << 20
        ),
        cost_estimate=pl.CostEstimate(
            flops=4 * heads * total_rows * length * dim,
            bytes_accessed=4 * heads * length * dim,
            transcendentals=heads * total_rows * length,
        ),
        name="prefix_attention",
    )(
        q,
        pltpu.with_memory_space_constraint(keys, pltpu.HBM),
        pltpu.with_memory_space_constraint(values, pltpu.HBM),
    )


def suffix_kernel(scale, lengths_ref, q_ref, k_ref, v_ref, o_ref, lse_ref):
    step = pl.program_id(0)
    count, heads, length = k_ref.shape[0], k_ref.shape[1], k_ref.shape[2]
    group = q_ref.shape[1] // heads
    sessions = pl.num_programs(0) * count
    pairs = [(s, h) for s in range(count) for h in range(heads)]
    all_scores = [
        lax.dot_general(
            q_ref[s, h * group : (h + 1) * group], k_ref[s, h], NT, preferred_element_type=F32
        )
        for s, h in pairs
    ]
    position = lax.broadcasted_iota(jnp.int32, (group, length), 1)
    softened = []
    for (s, h), scores in zip(pairs, all_scores):
        scores = jnp.where(position < lengths_ref[step * count + s], scores, -1e30)
        top = jnp.max(scores, axis=1, keepdims=True)
        weights = jnp.exp2((scores - top) * scale)
        softened.append((top, jnp.sum(weights, axis=1, keepdims=True), weights.astype(BF16)))
    for (s, h), (top, total, weights) in zip(pairs, softened):
        out = jnp.dot(weights, v_ref[s, h], preferred_element_type=F32) / total
        rows = pl.ds((h * sessions + step * count + s) * group, group)
        o_ref[rows, :] = out
        lse_ref[rows, :] = jnp.broadcast_to(top * scale + jnp.log2(total), out.shape)


def suffix_attention(q, keys, values, lengths, scale):
    sessions, heads, length, dim = keys.shape
    rows = q.shape[1] * sessions
    count = 4
    spec = pl.BlockSpec((rows, dim), lambda s, n: (0, 0))
    return pl.pallas_call(
        functools.partial(suffix_kernel, scale),
        grid_spec=pltpu.PrefetchScalarGridSpec(
            num_scalar_prefetch=1,
            grid=(sessions // count,),
            in_specs=[
                pl.BlockSpec((count,) + q.shape[1:], lambda s, n: (s, 0, 0)),
                pl.BlockSpec((count, heads, length, dim), lambda s, n: (s, 0, 0, 0)),
                pl.BlockSpec((count, heads, length, dim), lambda s, n: (s, 0, 0, 0)),
            ],
            out_specs=[spec, spec],
        ),
        out_shape=[jax.ShapeDtypeStruct((rows, dim), F32)] * 2,
        compiler_params=pltpu.CompilerParams(vmem_limit_bytes=16 << 20),
        cost_estimate=pl.CostEstimate(
            flops=4 * rows * length * dim,
            bytes_accessed=4 * sessions * heads * length * dim,
            transcendentals=rows * length,
        ),
        name="suffix_attention",
    )(
        lengths,
        q,
        pltpu.with_memory_space_constraint(keys, pltpu.HBM),
        pltpu.with_memory_space_constraint(values, pltpu.HBM),
    )


def merge_kernel(heads, parts_ref, suffix_ref, suffix_lse_ref, out_ref, result_ref):
    sources, padded, dim = parts_ref.shape
    rows = padded - 8
    copies, sessions, _ = out_ref.shape
    stats = []
    for c in range(sources):
        three = parts_ref[c, rows : rows + 8, :].astype(F32)
        stats.append(three[0:1] + three[1:2] + three[2:3])
    filler = jnp.full((rows - sources, rows), -3e38, F32)
    table = jnp.concatenate(stats + [filler], axis=0).T
    own = suffix_lse_ref[...]
    top = jnp.maximum(jnp.max(table, axis=1, keepdims=True), own[:, 0:1])
    shares = jnp.exp2(table - top)
    own_share = jnp.exp2(own[:, 0:1] - top)
    total = jnp.sum(shares, axis=1, keepdims=True) + own_share
    result = own_share * suffix_ref[...]
    for c in range(sources):
        result += shares[:, c : c + 1] * parts_ref[c, 0:rows, :].astype(F32)
    result_ref[...] = result / total
    group = rows // sessions // heads
    for h in range(heads):
        for g in range(group):
            first = h * sessions * group + g
            piece = result_ref[pl.ds(first, sessions, stride=group), :].astype(BF16)
            column = (h * group + g) * dim
            for copy in range(copies):
                out_ref[copy, :, column : column + dim] = piece


def merge(parts, suffix, suffix_lse, sessions, heads, copies):
    rows, dim = suffix.shape
    return pl.pallas_call(
        functools.partial(merge_kernel, heads),
        scratch_shapes=[pltpu.VMEM((rows, dim), F32)],
        compiler_params=pltpu.CompilerParams(vmem_limit_bytes=16 << 20),
        out_shape=jax.ShapeDtypeStruct((copies, sessions, rows // sessions * dim), BF16),
        name="merge_shards",
    )(parts, suffix, suffix_lse)


def project_kernel(place_ref, attended_ref, *refs):
    weights, out_ref = refs[:-1], refs[-1]
    heads, wide, rows, columns = out_ref.shape
    for k, weight_ref in enumerate(weights):
        product = jnp.dot(attended_ref[...], weight_ref[...], preferred_element_type=F32)
        x = lax.rem(place_ref[0] + (wide - k), wide)
        out_ref[:, x] = product.astype(BF16).reshape(heads, rows, columns)


def project(place, attended, weights, heads):
    sessions, features = attended.shape
    columns = weights[0].shape[1]
    vmem = pl.BlockSpec(memory_space=pltpu.VMEM)
    return pl.pallas_call(
        project_kernel,
        in_specs=[pl.BlockSpec(memory_space=pltpu.SMEM)] + [vmem] * (1 + len(weights)),
        out_specs=vmem,
        out_shape=jax.ShapeDtypeStruct((heads, len(weights), sessions // heads, columns), BF16),
        compiler_params=pltpu.CompilerParams(vmem_limit_bytes=16 << 20),
        name="project",
    )(place, attended, *weights)


def finish_kernel(parts_ref, out_ref):
    for x in range(parts_ref.shape[1]):
        total = parts_ref[0, x].astype(F32)
        for h in range(1, parts_ref.shape[0]):
            total += parts_ref[h, x].astype(F32)
        out_ref[:, x] = total


def finish(parts):
    _, x, outer, sessions, columns = parts.shape
    return pl.pallas_call(
        finish_kernel,
        out_shape=jax.ShapeDtypeStruct((outer, x, sessions, columns), F32),
        compiler_params=pltpu.CompilerParams(vmem_limit_bytes=16 << 20),
        name="sum_heads",
    )(parts)


def spread_kernel(q_ref, out_ref):
    copies, heads, rows, dim = out_ref.shape
    group = q_ref.shape[1] // heads
    for h in range(heads):
        q = q_ref[:, h * group : (h + 1) * group, :].reshape(rows, dim)
        for c in range(copies):
            out_ref[c, h] = q


def spread(queries, copies, heads):
    sessions, local_heads, dim = queries.shape
    shape = (copies, heads, sessions * local_heads // heads, dim)
    return pl.pallas_call(
        spread_kernel,
        out_shape=jax.ShapeDtypeStruct(shape, queries.dtype),
        name="spread_queries",
    )(queries)


def per_device(queries, prefix_keys, prefix_values, suffix_keys, suffix_values, lengths, out_weight):
    sessions, local_heads, dim = queries.shape
    kv_local = prefix_keys.shape[0]
    scale = LOG2E / math.sqrt(dim)
    ctx = lax.axis_size("ctx")
    heads = lax.axis_size("yh") * lax.axis_size("core")
    wide = lax.axis_size("x")
    low = lax.axis_size("yl")

    gathered = lax.all_to_all(spread(queries, ctx, kv_local), "ctx", 0, 0, tiled=False)
    weights = [out_weight]
    for k in range(1, wide):
        pairs = [(x, (x + k) % wide) for x in range(wide)]
        weights.append(lax.ppermute(out_weight, "x", pairs))

    parts = prefix_attention(gathered, prefix_keys, prefix_values, scale)
    place = lax.axis_index("x").astype(jnp.int32).reshape(1)
    parts, queries, place = lax.optimization_barrier((parts, queries, place))
    parts = lax.all_to_all(parts, "ctx", 0, 0, tiled=True)
    suffix, suffix_lse = suffix_attention(queries, suffix_keys, suffix_values, lengths, scale)

    group = ctx * low
    everyone = merge(parts, suffix, suffix_lse, sessions, kv_local, group)
    everyone, weights, place = lax.optimization_barrier((everyone, weights, place))
    everyone = lax.all_to_all(everyone, ("ctx", "yl"), 0, 0, tiled=True)
    everyone = everyone.reshape(group * sessions, local_heads * dim)
    partial_out = project(place, everyone, weights, heads)
    partial_out = partial_out.reshape(heads * wide, group * sessions // heads, out_weight.shape[1])
    partial_out = lax.all_to_all(partial_out, ("yh", "core", "x"), 0, 0, tiled=True)
    partial_out = partial_out.reshape(heads, wide, group // heads, sessions, out_weight.shape[1])
    return finish(partial_out).reshape(group * sessions * wide // heads, out_weight.shape[1])


def solution(mesh):
    fine = Mesh(mesh.devices.reshape(8, 2, 2, 2, 4), ("ctx", "yh", "core", "yl", "x"))
    both = ("ctx",) + SESS
    return jax.shard_map(
        per_device,
        mesh=fine,
        in_specs=(
            P(both, HEAD, None),
            P(HEAD, "ctx", None),
            P(HEAD, "ctx", None),
            P(both, HEAD, None, None),
            P(both, HEAD, None, None),
            P(both),
            P(HEAD, both),
        ),
        out_specs=P(HEAD, both),
        check_vma=False,
    )
```
